256 devices in a mesh: au: 8 (over y, z_lo), ia: 32 (over z_hi, x, core).
Axes of the slice: x: 4, y: 4, z: 8 (z_hi: 4, z_lo: 2; z = z_hi * 2 + z_lo), core: 2. Of those that a mesh axis runs over, the one named last changes fastest.
Arguments:
- user_factors: bfloat16 [8192, 256], P(('au', 'ia')), may hold values from -6 to 6
- item_factors: bfloat16 [131072, 256], P(('ia', 'au')), may hold values from -6 to 6
- user_tangent: bfloat16 [8192, 256], P(('au', 'ia')), may hold values from -6 to 6
- item_tangent: bfloat16 [131072, 256], P(('ia', 'au')), may hold values from -6 to 6
- block_mask: int32 [64, 1024], P('au', 'ia'), may hold values from 0 to 1, as said below
Outputs:
- user_product: float32 [8192, 256], P(('au', 'ia'))
- item_product: float32 [131072, 256], P(('ia', 'au'))
The draws below stay inside these ranges and needn't reach their ends.
Inputs may be any that keep to these rules, and one draw needn't show every extreme that they name: `block_mask`: users are grouped in runs of 32 * 32 and items in runs of 512 * 8; where one user group meets one item group, at most 128 of its 8 x 32 blocks are observed, and in every draw one such meeting has exactly 128.
All inputs are finite; a program needn't handle non-finite values.
Results may differ from the reference program's by a relative error of at most 0.0013.
Values may be sent and summed in bfloat16 or wider, within the bound.
A program may use at most 64 MiB of HBM per device.

```python
import jax
import jax.numpy as jnp
from jax import lax

R = 256
US_DEV = 32
IT_DEV = 512
USERS = 8192
ITEMS = 131072
ROWBLK = 8
COLBLK = 32
UBLK = 64
IBLK = 1024
MAXB = 128
N_AU = 8
N_IA = 32


def draw_block_mask(key, part):
    key_count = jax.random.fold_in(key, 11)
    key_heavy = jax.random.fold_in(key, 12)
    key_place = jax.random.fold_in(key, 13)
    regions = N_AU * N_IA
    region_size = ROWBLK * COLBLK
    counts = jax.random.randint(key_count, (regions,), MAXB // 8, MAXB * 7 // 8 + 1)
    heavy = jax.random.randint(key_heavy, (), 0, regions)
    counts = jnp.where(jnp.arange(regions) == heavy, MAXB, counts)
    region_keys = jax.random.split(key_place, regions)
    places = jax.vmap(lambda k: jax.random.permutation(k, region_size))(region_keys)
    marks = (places < counts[:, None]).astype(jnp.int32)
    marks = marks.reshape(N_AU, N_IA, ROWBLK, COLBLK)
    marks = jnp.transpose(marks, (0, 2, 1, 3))
    return marks.reshape(UBLK, IBLK)


def block_scale(rng, shape, cuts, smallest, largest):
    level = 1.0
    for dim, blocks in cuts:
        steps = jax.random.uniform(jax.random.fold_in(jax.random.fold_in(rng, 6), dim), (blocks,), jnp.float32, smallest / len(cuts), largest / len(cuts))
        level = level * jnp.repeat(jnp.exp(steps), shape[dim] // blocks).reshape((-1,) + (1,) * (len(shape) - 1 - dim))
    return level


def bell_draw(own_key, extent, scale, limit, pieces=(), kind=jnp.bfloat16):
    loudness = block_scale(own_key, extent, pieces, -0.22, 0.18) if pieces else 1.0
    entries = jax.random.normal(own_key, extent, jnp.float32) * scale * loudness
    return jnp.minimum(jnp.maximum(entries, -limit), limit).astype(kind)


def setup_inputs(seed: int = 0) -> dict:
    splits = jax.random.split(jax.random.key(seed), 6)
    return {
        "user_factors": bell_draw(splits[0], (USERS, R), 1.0, 6.0, ((0, 256),)),
        "item_factors": bell_draw(splits[1], (ITEMS, R), 1.0, 6.0, ((0, 256),)),
        "user_tangent": bell_draw(splits[2], (USERS, R), 1.0, 6.0, ((0, 256),)),
        "item_tangent": bell_draw(splits[3], (ITEMS, R), 1.0, 6.0, ((0, 256),)),
        "block_mask": draw_block_mask(jax.random.fold_in(splits[5], 71), 0),
    }


batch_blocks = 16

def region_pass(users, user_tan, items, item_tan, mask_part):
    row_blocks, col_blocks = mask_part.shape
    block_rows = users.shape[0] // row_blocks
    width = users.shape[1]
    user_tiles = users.reshape(row_blocks, block_rows, width)
    utan_tiles = user_tan.reshape(row_blocks, block_rows, width)
    item_tiles = items.reshape(col_blocks, block_rows, width)
    itan_tiles = item_tan.reshape(col_blocks, block_rows, width)
    total = row_blocks * col_blocks
    flat = mask_part.reshape(-1).astype(jnp.int32)
    index = jnp.arange(total, dtype=jnp.int32)
    order = jnp.argsort((1 - flat) * total + index).astype(jnp.int32)
    live = flat[order].astype(jnp.float32)
    order = jnp.concatenate([order, jnp.zeros((batch_blocks,), jnp.int32)])
    live = jnp.concatenate([live, jnp.zeros((batch_blocks,), jnp.float32)])
    row_ids = (order // col_blocks).astype(jnp.int32)
    col_ids = (order % col_blocks).astype(jnp.int32)
    scaling = 1.0 / jnp.sqrt(jnp.float32(width))
    turns = -(-total // batch_blocks)

    def one_turn(turn, carry):
        acc_user, acc_item = carry
        first = (turn * batch_blocks).astype(jnp.int32)
        rsel = lax.dynamic_slice_in_dim(row_ids, first, batch_blocks)
        csel = lax.dynamic_slice_in_dim(col_ids, first, batch_blocks)
        lsel = lax.dynamic_slice_in_dim(live, first, batch_blocks)
        urow = user_tiles[rsel].astype(jnp.float32)
        durow = utan_tiles[rsel].astype(jnp.float32)
        vrow = item_tiles[csel].astype(jnp.float32)
        dvrow = itan_tiles[csel].astype(jnp.float32)
        score = jnp.einsum('gar,gbr->gab', urow, vrow) * scaling
        prob = jax.nn.sigmoid(score)
        weight = prob * (1.0 - prob)
        tang = (jnp.einsum('gar,gbr->gab', durow, vrow) + jnp.einsum('gar,gbr->gab', urow, dvrow)) * scaling
        curv = (lsel[:, None, None] * weight * tang).astype(jnp.bfloat16).astype(jnp.float32)
        to_user = jnp.einsum('gab,gbr->gar', curv, vrow)
        to_item = jnp.einsum('gab,gar->gbr', curv, urow)
        onehot_rows = (rsel[:, None] == jnp.arange(row_blocks, dtype=jnp.int32)[None, :]).astype(jnp.float32)
        onehot_cols = (csel[:, None] == jnp.arange(col_blocks, dtype=jnp.int32)[None, :]).astype(jnp.float32)
        acc_user = acc_user + jnp.einsum('gk,gar->kar', onehot_rows, to_user, precision=lax.Precision.HIGHEST)
        acc_item = acc_item + jnp.einsum('gk,gbr->kbr', onehot_cols, to_item, precision=lax.Precision.HIGHEST)
        return (acc_user, acc_item)
    start = (jnp.zeros((row_blocks, block_rows, width), jnp.float32), jnp.zeros((col_blocks, block_rows, width), jnp.float32))
    acc_user, acc_item = lax.fori_loop(0, turns, one_turn, start)
    return ((acc_user * scaling).reshape(-1, width), (acc_item * scaling).reshape(-1, width))

def reference(user_factors, item_factors, user_tangent, item_tangent, block_mask):
    group_rows = US_DEV * N_IA
    column_rows = IT_DEV * N_AU

    def per_group(carry, group):
        users = lax.dynamic_slice_in_dim(user_factors, group * group_rows, group_rows, 0)
        user_tan = lax.dynamic_slice_in_dim(user_tangent, group * group_rows, group_rows, 0)
        masks = lax.dynamic_slice_in_dim(block_mask, group * ROWBLK, ROWBLK, 0)

        def per_column(column):
            items = lax.dynamic_slice_in_dim(item_factors, column * column_rows, column_rows, 0)
            item_tan = lax.dynamic_slice_in_dim(item_tangent, column * column_rows, column_rows, 0)
            mask_part = lax.dynamic_slice_in_dim(masks, column * COLBLK, COLBLK, 1)
            return region_pass(users, user_tan, items, item_tan, mask_part)
        part_user, part_item = lax.map(per_column, jnp.arange(N_IA, dtype=jnp.int32))
        return (carry + part_item.reshape(ITEMS, R), lax.optimization_barrier(jnp.sum(part_user, axis=0)))
    item_total, user_parts = lax.scan(per_group, jnp.zeros((ITEMS, R), jnp.float32), jnp.arange(N_AU, dtype=jnp.int32))
    return (user_parts.reshape(USERS, R), item_total)
```

```python
import jax
import jax.numpy as jnp
from jax import lax
from jax.experimental import pallas as pl
from jax.experimental.pallas import tpu as pltpu
from jax.sharding import PartitionSpec as P

MESH = pl.DeviceIdType.MESH
NT = (((1,), (1,)), ((), ()))
TN = (((0,), (0,)), ((), ()))
NN = (((1,), (0,)), ((), ()))
ORDER = (0, 1, 3, 2)
N_SEM = 96


def dot(a, b, dims):
    return lax.dot_general(a, b, dims, preferred_element_type=jnp.float32)


def kernel(
    uf, ut, vf, vt, mask, ou, oi,
    G, Z, mb, Mx, PU, PV, R1, S1, R2, S2, R3, RI1, SI, RI2, send, recv,
):
    au, ia = lax.axis_index("au"), lax.axis_index("ia")
    y, zl = lax.div(au, 2), lax.rem(au, 2)
    zh, x, c = lax.div(ia, 8), lax.rem(lax.div(ia, 2), 4), lax.rem(ia, 2)
    rows = uf.shape[0]
    items, width = vf.shape

    def dev(dx=0, dy=0, dz=0, sib=False, mate=False):
        z = 1 - zl if mate else zl
        core = 1 - c if sib else c
        return (
            lax.rem(y + dy, 4) * 2 + z,
            (lax.rem(zh + dz, 4) * 4 + lax.rem(x + dx, 4)) * 2 + core,
        )

    partners = [dev(sib=True), dev(mate=True)]
    for d in (1, 2, 3):
        partners += [dev(dx=d), dev(dy=d), dev(dz=d)]
    barrier = pltpu.get_barrier_semaphore()
    for p in partners:
        pl.semaphore_signal(barrier, inc=1, device_id=p, device_id_type=MESH)

    G[0, 0, :, :width] = ut[...]
    G[0, 0, :, width:] = uf[...]
    Z[0, :, :width] = vf[...]
    Z[0, :, width:] = vt[...]
    mb[0, 0] = jnp.zeros(mb.shape[2:], jnp.float32)
    mb[0, 0, :, : mask.shape[1]] = mask[...].astype(jnp.float32)

    made = []

    def copy(src, dst, device):
        i = len(made)
        made.append(
            pltpu.make_async_remote_copy(
                src_ref=src,
                dst_ref=dst,
                send_sem=send.at[i],
                recv_sem=recv.at[i],
                device_id=device,
                device_id_type=MESH,
            )
        )
        return made[-1]

    def along(axis, d):
        return dev(dx=d) if axis == 0 else dev(dy=d)

    far = (1, 3, 2)
    by_z = {
        ORDER.index(4 - d): copy(G.at[0, 0], G.at[ORDER.index(4 - d), 0], dev(dz=d))
        for d in far
    }
    first = [
        [copy(G.at[k, 0], G.at[k, 4 - d], along(k % 2, d)) for d in far]
        for k in range(4)
    ]
    second = [
        [
            copy(
                G.at[k, pl.ds(0, 4)],
                G.at[k, pl.ds(4 * (4 - d), 4)],
                along(1 - k % 2, d),
            )
            for d in far
        ]
        for k in range(4)
    ]
    mask_y = [copy(mb.at[0, 0], mb.at[0, 4 - d], dev(dy=d)) for d in far]
    mask_c = copy(mb.at[0], mb.at[1], dev(sib=True))
    item_m = copy(Z.at[0], Z.at[2], dev(mate=True))
    item_s = copy(Z.at[0], Z.at[1], dev(sib=True))
    item_f = copy(Z.at[2], Z.at[3], dev(sib=True))
    back1 = [
        [
            copy(PU.at[k, pl.ds(4 * d, 4)], R1.at[k, d - 1], along(1 - k % 2, d))
            for d in far
        ]
        for k in range(4)
    ]
    back2 = [
        [copy(S1.at[k, d], R2.at[k, d - 1], along(k % 2, d)) for d in far]
        for k in range(4)
    ]
    back3 = [copy(S2.at[k], R3.at[k - 1], dev(dz=ORDER[k])) for k in (1, 2, 3)]
    sum_s0 = copy(PV.at[1], RI1.at[0], dev(sib=True))
    sum_s1 = copy(PV.at[3], RI1.at[1], dev(sib=True))
    sum_m = copy(SI, RI2, dev(mate=True))

    def start(copies):
        for cp in copies:
            cp.start()

    def arrive(copies):
        for cp in copies:
            cp.wait_recv()

    pl.semaphore_wait(barrier, len(partners))
    start(by_z[k] for k in (1, 2, 3))
    start(first[0])
    start(mask_y)
    item_m.start()
    item_s.start()
    PU[...] = jnp.zeros_like(PU)
    PV[...] = jnp.zeros_like(PV)
    for k in (1, 2):
        by_z[k].wait_recv()
        start(first[k])
    arrive(first[0])
    start(second[0])
    arrive(first[1])
    start(second[1])
    by_z[3].wait_recv()
    start(first[3])
    arrive(mask_y)
    mask_c.start()
    arrive(first[2])
    start(second[2])
    arrive(first[3])
    start(second[3])
    mask_c.wait_recv()

    for p in range(2):
        zone = zl if p == 0 else 1 - zl
        j = lax.broadcasted_iota(jnp.int32, (128, items), 0)
        l = lax.broadcasted_iota(jnp.int32, (128, items), 1)
        pick = (j == 4 * (y * 2 + zone) + l // 128).astype(jnp.bfloat16)
        for cc in range(2):
            seen = dot(mb[cc].reshape(32, 128).astype(jnp.bfloat16), pick, NN)
            seen = seen.astype(jnp.bfloat16)
            for k in range(4):
                slot = lax.broadcasted_iota(jnp.int32, (128, 32), 0) // 8
                row = lax.broadcasted_iota(jnp.int32, (128, 32), 1)
                hi, lo = slot // 4, slot % 4
                dy, dx = (hi, lo) if k % 2 == 0 else (lo, hi)
                block = lax.rem(zh + ORDER[k], 4) * 2 + ((x + dx) % 4) // 2
                put = (row == dy * 8 + block).astype(jnp.bfloat16)
                Mx[k, p, :, :, pl.ds(cc * items, items)] = dot(put, seen, NN).reshape(
                    16, 8, items
                )
    item_s.wait_recv()

    def sum1(k):
        arrive(back1[k])
        S1[k] = (PU[k, pl.ds(0, 4)] + R1[k, 0]) + (R1[k, 1] + R1[k, 2])
        start(back2[k])

    def sum2(k):
        arrive(back2[k])
        S2[k] = (S1[k, 0] + R2[k, 0]) + (R2[k, 1] + R2[k, 2])
        if k:
            back3[k - 1].start()

    def step(i, carry):
        p, k = lax.div(i, 4), lax.rem(i, 4)
        for n in range(4):
            @pl.when(i == n)
            def _():
                arrive(second[n])

        @pl.when(i == 4)
        def _():
            item_f.wait_recv()

        w = G[k].reshape(16 * rows, 2 * width)
        z = Z[pl.ds(2 * p, 2)].reshape(2 * items, 2 * width)
        s = dot(w[:, width:], z[:, :width], NT)
        t = dot(w, z, NT)
        e = jnp.exp(jnp.abs(s) * (-1.0 / 16.0))
        r = 1.0 / (1.0 + e)
        cu = (e * r * r * t).reshape(16, 4, 8, 2 * items) * Mx[k, p][:, None]
        cu = cu.reshape(16 * rows, 2 * items).astype(jnp.bfloat16)
        PU[k] += dot(cu, z[:, :width], NN).reshape(16, rows, width)
        PV[pl.ds(2 * p, 2)] += dot(cu, w[:, width:], TN).reshape(2, items, width)

        @pl.when(i == 2)
        def _():
            item_m.wait_recv()
            item_f.start()

        @pl.when(i == 3)
        def _():
            sum_s0.start()

        for n in range(4):
            @pl.when(i == 4 + n)
            def _():
                start(back1[n])

        @pl.when(i == 6)
        def _():
            sum1(0)

        return carry

    lax.fori_loop(0, 8, step, 0)
    sum_s1.start()
    sum1(1)
    sum_s1.wait_recv()
    SI[...] = PV[2] + RI1[1]
    sum_m.start()
    sum2(0)
    sum2(1)
    sum1(2)
    sum1(3)
    sum2(2)
    sum2(3)
    arrive(back3)
    out = 1.0 / 256.0
    ou[...] = ((S2[0] + R3[0]) + (R3[1] + R3[2])) * out
    sum_s0.wait_recv()
    sum_m.wait_recv()
    oi[...] = (PV[0] + RI1[0] + RI2[...]) * out
    for cp in made:
        cp.wait_send()


def on_device(user_factors, item_factors, user_tangent, item_tangent, block_mask):
    rows, width = user_factors.shape
    items = item_factors.shape[0]
    f32, bf16 = jnp.float32, jnp.bfloat16
    vmem = pl.BlockSpec(memory_space=pltpu.VMEM)
    scratch = [
        pltpu.VMEM((4, 16, rows, 2 * width), bf16),
        pltpu.VMEM((4, items, 2 * width), bf16),
        pltpu.VMEM((2, 4, 8, 128), f32),
        pltpu.VMEM((4, 2, 16, 8, 2 * items), f32),
        pltpu.VMEM((4, 16, rows, width), f32),
        pltpu.VMEM((4, items, width), f32),
        pltpu.VMEM((4, 3, 4, rows, width), f32),
        pltpu.VMEM((4, 4, rows, width), f32),
        pltpu.VMEM((4, 3, rows, width), f32),
        pltpu.VMEM((4, rows, width), f32),
        pltpu.VMEM((3, rows, width), f32),
        pltpu.VMEM((2, items, width), f32),
        pltpu.VMEM((items, width), f32),
        pltpu.VMEM((items, width), f32),
        pltpu.SemaphoreType.DMA((N_SEM,)),
        pltpu.SemaphoreType.DMA((N_SEM,)),
    ]
    return pl.pallas_call(
        kernel,
        out_shape=(
            jax.ShapeDtypeStruct((rows, width), f32),
            jax.ShapeDtypeStruct((items, width), f32),
        ),
        in_specs=[vmem] * 5,
        out_specs=[vmem] * 2,
        scratch_shapes=scratch,
        compiler_params=pltpu.CompilerParams(
            collective_id=0, has_side_effects=True, vmem_limit_bytes=56 << 20
        ),
    )(user_factors, user_tangent, item_factors, item_tangent, block_mask)


def solution(mesh):
    placed = (
        P(("au", "ia"), None),
        P(("ia", "au"), None),
        P(("au", "ia"), None),
        P(("ia", "au"), None),
        P("au", "ia"),
    )
    return jax.shard_map(
        on_device,
        mesh=mesh,
        in_specs=placed,
        out_specs=(P(("au", "ia"), None), P(("ia", "au"), None)),
        check_vma=False,
    )
```

```python
import jax
import jax.numpy as jnp
from jax import lax
from jax.experimental import pallas as pl
from jax.experimental.pallas import tpu as pltpu
from jax.sharding import PartitionSpec as P

MESH = pl.DeviceIdType.MESH
NT = (((1,), (1,)), ((), ()))
TN = (((0,), (0,)), ((), ()))
NN = (((1,), (0,)), ((), ()))
ORDER = (0, 1, 3, 2)
N_SEM = 112


def dot(a, b, dims):
    return lax.dot_general(a, b, dims, preferred_element_type=jnp.float32)


def kernel(
    uf, ut, vf, vt, mask, ou, oi,
    G, Z, mi, mb, Mx, PU, PV, R1, S1, R2, S2, R3, RI1, SI, RI2, send, recv, local,
):
    au, ia = lax.axis_index("au"), lax.axis_index("ia")
    y, zl = lax.div(au, 2), lax.rem(au, 2)
    zh, x, c = lax.div(ia, 8), lax.rem(lax.div(ia, 2), 4), lax.rem(ia, 2)
    rows, width = uf.shape
    items = vf.shape[0]
    half = rows // 2

    def dev(dx=0, dy=0, dz=0, sib=False, mate=False):
        z = 1 - zl if mate else zl
        core = 1 - c if sib else c
        return (
            lax.rem(y + dy, 4) * 2 + z,
            (lax.rem(zh + dz, 4) * 4 + lax.rem(x + dx, 4)) * 2 + core,
        )

    partners = [dev(sib=True), dev(mate=True)]
    for d in (1, 2, 3):
        partners += [dev(dx=d), dev(dy=d), dev(dz=d)]
    barrier = pltpu.get_barrier_semaphore()
    for p in partners:
        pl.semaphore_signal(barrier, inc=1, device_id=p, device_id_type=MESH)

    left, right = pl.ds(0, width), pl.ds(width, width)
    place = [
        pltpu.make_async_copy(ut, G.at[0, 0, 0, :, left], local.at[0]),
        pltpu.make_async_copy(uf, G.at[0, 0, 0, :, right], local.at[1]),
        pltpu.make_async_copy(mask, mi, local.at[2]),
        pltpu.make_async_copy(vf, Z.at[0, :, left], local.at[3]),
        pltpu.make_async_copy(vt, Z.at[0, :, right], local.at[4]),
    ]
    for cp in place:
        cp.start()

    made = []

    def copy(src, dst, device):
        i = len(made)
        made.append(
            pltpu.make_async_remote_copy(
                src_ref=src,
                dst_ref=dst,
                send_sem=send.at[i],
                recv_sem=recv.at[i],
                device_id=device,
                device_id_type=MESH,
            )
        )
        return made[-1]

    far = (1, 3, 2)
    h0, h1 = pl.ds(0, half), pl.ds(half, half)
    al = pl.ds(0, 4)
    by_z = {
        ORDER.index(4 - d): copy(
            G.at[0, 0, 0], G.at[ORDER.index(4 - d), 0, 0], dev(dz=d)
        )
        for d in far
    }
    first, second = [], []
    for k in range(4):
        first.append((
            [copy(G.at[k, 0, 0, h0], G.at[k, 0, 4 - d, h0], dev(dx=d)) for d in far],
            [copy(G.at[k, 0, 0, h1], G.at[k, 4 - d, 0, h1], dev(dy=d)) for d in far],
        ))
        second.append((
            [copy(G.at[k, 0, al, h0], G.at[k, 4 - d, al, h0], dev(dy=d)) for d in far],
            [copy(G.at[k, al, 0, h1], G.at[k, al, 4 - d, h1], dev(dx=d)) for d in far],
        ))
    mask_y = [copy(mb.at[0, 0], mb.at[0, 4 - d], dev(dy=d)) for d in far]
    mask_c = copy(mb.at[0], mb.at[1], dev(sib=True))
    item_m = copy(Z.at[0], Z.at[2], dev(mate=True))
    item_s = copy(Z.at[0], Z.at[1], dev(sib=True))
    item_f = copy(Z.at[2], Z.at[3], dev(sib=True))
    back1, back2 = [], []
    for k in range(4):
        back1.append((
            [copy(PU.at[k, d, al, h0], R1.at[k, d - 1, 0], dev(dy=d)) for d in far],
            [copy(PU.at[k, al, d, h1], R1.at[k, d - 1, 1], dev(dx=d)) for d in far],
        ))
        back2.append((
            [copy(S1.at[k, 0, d], R2.at[k, d - 1, 0], dev(dx=d)) for d in far],
            [copy(S1.at[k, 1, d], R2.at[k, d - 1, 1], dev(dy=d)) for d in far],
        ))
    back3 = [copy(S2.at[k], R3.at[k - 1], dev(dz=ORDER[k])) for k in (1, 2, 3)]
    sum_s0 = copy(PV.at[1], RI1.at[0], dev(sib=True))
    sum_s1 = copy(PV.at[3], RI1.at[1], dev(sib=True))
    sum_m = copy(SI, RI2, dev(mate=True))

    def start(copies):
        for cp in copies:
            cp.start()

    def arrive(copies):
        for cp in copies:
            cp.wait_recv()

    def begin(pair):
        start(pair[0])
        start(pair[1])

    def after(came, then):
        for n in range(2):
            arrive(came[n])
            start(then[n])

    place[0].wait()
    place[1].wait()
    pl.semaphore_wait(barrier, len(partners))
    start(by_z[k] for k in (1, 2, 3))
    begin(first[0])
    place[3].wait()
    place[4].wait()
    item_m.start()
    item_s.start()
    place[2].wait()
    mb[0, 0] = jnp.zeros(mb.shape[2:], jnp.float32)
    mb[0, 0, :, : mask.shape[1]] = mi[...].astype(jnp.float32)
    start(mask_y)
    PU[...] = jnp.zeros_like(PU)
    PV[...] = jnp.zeros_like(PV)
    by_z[1].wait_recv()
    begin(first[1])
    by_z[2].wait_recv()
    begin(first[2])
    after(first[0], second[0])
    by_z[3].wait_recv()
    begin(first[3])
    arrive(mask_y)
    mask_c.start()
    after(first[1], second[1])
    after(first[2], second[2])
    after(first[3], second[3])
    mask_c.wait_recv()

    for p in range(2):
        zone = zl if p == 0 else 1 - zl
        j = lax.broadcasted_iota(jnp.int32, (128, items), 0)
        l = lax.broadcasted_iota(jnp.int32, (128, items), 1)
        pick = (j == 4 * (y * 2 + zone) + l // 128).astype(jnp.bfloat16)
        for cc in range(2):
            seen = dot(mb[cc].reshape(32, 128).astype(jnp.bfloat16), pick, NN)
            seen = seen.astype(jnp.bfloat16)
            for k in range(4):
                slot = lax.broadcasted_iota(jnp.int32, (128, 32), 0) // 8
                row = lax.broadcasted_iota(jnp.int32, (128, 32), 1)
                dy, dx = slot // 4, slot % 4
                block = lax.rem(zh + ORDER[k], 4) * 2 + ((x + dx) % 4) // 2
                put = (row == dy * 8 + block).astype(jnp.bfloat16)
                Mx[k, p, :, :, pl.ds(cc * items, items)] = dot(put, seen, NN).reshape(
                    16, 8, items
                )
    item_s.wait_recv()

    def sum1(k):
        own = (PU[k, 0, :, h0], PU[k, :, 0, h1])
        for n in range(2):
            arrive(back1[k][n])
            S1[k, n] = (own[n] + R1[k, 0, n]) + (R1[k, 1, n] + R1[k, 2, n])
            start(back2[k][n])

    def sum2(k):
        for n, h in ((0, h0), (1, h1)):
            arrive(back2[k][n])
            S2[k, h] = (S1[k, n, 0] + R2[k, 0, n]) + (R2[k, 1, n] + R2[k, 2, n])
        if k:
            back3[k - 1].start()

    tile = items // 2

    def step(i, carry):
        p = lax.div(i, 4)
        k = lax.rem(i + p, 4)
        for n in range(4):
            @pl.when(i == n)
            def _():
                arrive(second[n][0])
                arrive(second[n][1])

        @pl.when(i == 4)
        def _():
            item_f.wait_recv()

        w = G[k].reshape(16 * rows, 2 * width)

        def front(q):
            z = Z[2 * p + q // 2, pl.ds((q % 2) * tile, tile)]
            return z, dot(w[:, width:], z[:, :width], NT), dot(w, z, NT)

        def rear(q, z, s, t):
            e = jnp.exp(jnp.abs(s) * (-1.0 / 16.0))
            r = 1.0 / (1.0 + e)
            seen = Mx[k, p, :, :, pl.ds(q * tile, tile)]
            cu = (e * r * r * t).reshape(16, rows // 8, 8, tile) * seen[:, None]
            cu = cu.reshape(16 * rows, tile).astype(jnp.bfloat16)
            PV[2 * p + q // 2, pl.ds((q % 2) * tile, tile)] += dot(cu, w[:, width:], TN)
            return dot(cu, z[:, :width], NN)

        total, held = None, front(0)
        for q in range(4):
            now = held
            if q < 3:
                held = front(q + 1)
            part = rear(q, *now)
            total = part if total is None else total + part
        PU[k] += total.reshape(4, 4, rows, width)

        @pl.when(i == 2)
        def _():
            item_m.wait_recv()
            item_f.start()

        @pl.when(i == 3)
        def _():
            sum_s0.start()

        for n in range(4):
            @pl.when(i == 4 + n)
            def _():
                if n == 3:
                    sum_s1.start()
                begin(back1[(n + 1) % 4])

        return carry

    lax.fori_loop(0, 8, step, 0)
    sum_s1.wait_recv()
    SI[...] = PV[2] + RI1[1]
    sum_m.start()
    sum1(1)
    sum1(2)
    sum2(1)
    sum1(3)
    sum2(2)
    sum1(0)
    sum2(3)
    sum2(0)
    arrive(back3)
    out = 1.0 / 256.0
    ou[...] = ((S2[0] + R3[0]) + (R3[1] + R3[2])) * out
    sum_s0.wait_recv()
    sum_m.wait_recv()
    oi[...] = (PV[0] + RI1[0] + RI2[...]) * out
    for cp in made:
        cp.wait_send()


def on_device(user_factors, item_factors, user_tangent, item_tangent, block_mask):
    rows, width = user_factors.shape
    items = item_factors.shape[0]
    f32, bf16 = jnp.float32, jnp.bfloat16
    vmem = pl.BlockSpec(memory_space=pltpu.VMEM)
    scratch = [
        pltpu.VMEM((4, 4, 4, rows, 2 * width), bf16),
        pltpu.VMEM((4, items, 2 * width), bf16),
        pltpu.VMEM(block_mask.shape, jnp.int32),
        pltpu.VMEM((2, 4, 8, 128), f32),
        pltpu.VMEM((4, 2, 16, 8, 2 * items), f32),
        pltpu.VMEM((4, 4, 4, rows, width), f32),
        pltpu.VMEM((4, items, width), f32),
        pltpu.VMEM((4, 3, 2, 4, rows // 2, width), f32),
        pltpu.VMEM((4, 2, 4, rows // 2, width), f32),
        pltpu.VMEM((4, 3, 2, rows // 2, width), f32),
        pltpu.VMEM((4, rows, width), f32),
        pltpu.VMEM((3, rows, width), f32),
        pltpu.VMEM((2, items, width), f32),
        pltpu.VMEM((items, width), f32),
        pltpu.VMEM((items, width), f32),
        pltpu.SemaphoreType.DMA((N_SEM,)),
        pltpu.SemaphoreType.DMA((N_SEM,)),
        pltpu.SemaphoreType.DMA((5,)),
    ]
    return pl.pallas_call(
        kernel,
        out_shape=(
            jax.ShapeDtypeStruct((rows, width), f32),
            jax.ShapeDtypeStruct((items, width), f32),
        ),
        in_specs=[pl.BlockSpec(memory_space=pl.ANY)] * 5,
        out_specs=[vmem] * 2,
        scratch_shapes=scratch,
        compiler_params=pltpu.CompilerParams(
            collective_id=0, has_side_effects=True, vmem_limit_bytes=40 << 20
        ),
    )(user_factors, user_tangent, item_factors, item_tangent, block_mask)


def solution(mesh):
    placed = (
        P(("au", "ia"), None),
        P(("ia", "au"), None),
        P(("au", "ia"), None),
        P(("ia", "au"), None),
        P("au", "ia"),
    )
    return jax.shard_map(
        on_device,
        mesh=mesh,
        in_specs=placed,
        out_specs=(P(("au", "ia"), None), P(("ia", "au"), None)),
        check_vma=False,
    )
```

```python
import jax
import jax.numpy as jnp
from jax import lax
from jax.experimental import pallas as pl
from jax.experimental.pallas import tpu as pltpu
from jax.sharding import PartitionSpec as P

MESH = pl.DeviceIdType.MESH
NT = (((1,), (1,)), ((), ()))
TN = (((0,), (0,)), ((), ()))
NN = (((1,), (0,)), ((), ()))
ORDER = (0, 1, 3, 2)
N_SEM = 144


def dot(a, b, dims):
    return lax.dot_general(a, b, dims, preferred_element_type=jnp.float32)


def kernel(
    uf, ut, vf, vt, mask, ou, oi,
    G, Z, mi, mb, Mx, PU, PV, Q1, F1, R1, E1, S1, R2, S2, R3, RI1, QI, FI, R4, E4, send, recv, local,
):
    au, ia = lax.axis_index("au"), lax.axis_index("ia")
    y, zl = lax.div(au, 2), lax.rem(au, 2)
    zh, x, c = lax.div(ia, 8), lax.rem(lax.div(ia, 2), 4), lax.rem(ia, 2)
    rows, width = uf.shape
    items = vf.shape[0]
    half = rows // 2

    def dev(dx=0, dy=0, dz=0, sib=False, mate=False):
        z = 1 - zl if mate else zl
        core = 1 - c if sib else c
        return (
            lax.rem(y + dy, 4) * 2 + z,
            (lax.rem(zh + dz, 4) * 4 + lax.rem(x + dx, 4)) * 2 + core,
        )

    partners = [dev(sib=True), dev(mate=True)]
    for d in (1, 2, 3):
        partners += [dev(dx=d), dev(dy=d), dev(dz=d)]
    barrier = pltpu.get_barrier_semaphore()
    for p in partners:
        pl.semaphore_signal(barrier, inc=1, device_id=p, device_id_type=MESH)

    left, right = pl.ds(0, width), pl.ds(width, width)
    place = [
        pltpu.make_async_copy(ut, G.at[0, 0, 0, :, left], local.at[0]),
        pltpu.make_async_copy(uf, G.at[0, 0, 0, :, right], local.at[1]),
        pltpu.make_async_copy(mask, mi, local.at[2]),
        pltpu.make_async_copy(vf, Z.at[0, :, left], local.at[3]),
        pltpu.make_async_copy(vt, Z.at[0, :, right], local.at[4]),
    ]
    for cp in place:
        cp.start()

    made = []

    def copy(src, dst, device):
        i = len(made)
        made.append(
            pltpu.make_async_remote_copy(
                src_ref=src,
                dst_ref=dst,
                send_sem=send.at[i],
                recv_sem=recv.at[i],
                device_id=device,
                device_id_type=MESH,
            )
        )
        return made[-1]

    far = (1, 3, 2)
    h0, h1 = pl.ds(0, half), pl.ds(half, half)
    al = pl.ds(0, 4)
    by_z = {
        ORDER.index(4 - d): copy(
            G.at[0, 0, 0], G.at[ORDER.index(4 - d), 0, 0], dev(dz=d)
        )
        for d in far
    }
    first, second = [], []
    for k in range(4):
        first.append((
            [copy(G.at[k, 0, 0, h0], G.at[k, 0, 4 - d, h0], dev(dx=d)) for d in far],
            [copy(G.at[k, 0, 0, h1], G.at[k, 4 - d, 0, h1], dev(dy=d)) for d in far],
        ))
        second.append((
            [copy(G.at[k, 0, al, h0], G.at[k, 4 - d, al, h0], dev(dy=d)) for d in far],
            [copy(G.at[k, al, 0, h1], G.at[k, al, 4 - d, h1], dev(dx=d)) for d in far],
        ))
    mask_y = [copy(mb.at[0, 0], mb.at[0, 4 - d], dev(dy=d)) for d in far]
    mask_c = copy(mb.at[0], mb.at[1], dev(sib=True))
    item_m = copy(Z.at[0], Z.at[2], dev(mate=True))
    item_s = copy(Z.at[0], Z.at[1], dev(sib=True))
    item_f = copy(Z.at[2], Z.at[3], dev(sib=True))
    back1, back2 = [], []
    for k in range(4):
        pairs = []
        for n in range(2):
            pairs.append([])
            for d in far:
                to, at = (dev(dx=d) if n else dev(dy=d)), (k, n, d - 1)
                pairs[n].append(copy(F1.at[at], E1.at[at], to))
                pairs[n].append(copy(Q1.at[at], R1.at[at], to))
        back1.append(pairs)
        back2.append((
            [copy(S1.at[k, 0, d], R2.at[k, d - 1, 0], dev(dx=d)) for d in far],
            [copy(S1.at[k, 1, d], R2.at[k, d - 1, 1], dev(dy=d)) for d in far],
        ))
    back3 = [copy(S2.at[k], R3.at[k - 1], dev(dz=ORDER[k])) for k in (1, 2, 3)]
    sum_s0 = copy(PV.at[1], RI1.at[0], dev(sib=True))
    sum_s1 = copy(PV.at[3], RI1.at[1], dev(sib=True))
    sum_m = [copy(FI, E4, dev(mate=True)), copy(QI, R4, dev(mate=True))]

    def start(copies):
        for cp in copies:
            cp.start()

    def arrive(copies):
        for cp in copies:
            cp.wait_recv()

    def begin(pair):
        start(pair[0])
        start(pair[1])

    def after(came, then):
        for n in range(2):
            arrive(came[n])
            start(then[n])

    place[0].wait()
    place[1].wait()
    pl.semaphore_wait(barrier, len(partners))
    start(by_z[k] for k in (1, 2, 3))
    begin(first[0])
    place[3].wait()
    place[4].wait()
    item_m.start()
    item_s.start()
    place[2].wait()
    mb[0, 0] = jnp.zeros(mb.shape[2:], jnp.float32)
    mb[0, 0, :, : mask.shape[1]] = mi[...].astype(jnp.float32)
    start(mask_y)
    PU[...] = jnp.zeros_like(PU)
    PV[...] = jnp.zeros_like(PV)
    by_z[1].wait_recv()
    begin(first[1])
    by_z[2].wait_recv()
    begin(first[2])
    after(first[0], second[0])
    by_z[3].wait_recv()
    begin(first[3])
    arrive(mask_y)
    mask_c.start()
    after(first[1], second[1])
    after(first[2], second[2])
    after(first[3], second[3])
    mask_c.wait_recv()

    for p in range(2):
        zone = zl if p == 0 else 1 - zl
        j = lax.broadcasted_iota(jnp.int32, (128, items), 0)
        l = lax.broadcasted_iota(jnp.int32, (128, items), 1)
        pick = (j == 4 * (y * 2 + zone) + l // 128).astype(jnp.bfloat16)
        for cc in range(2):
            seen = dot(mb[cc].reshape(32, 128).astype(jnp.bfloat16), pick, NN)
            seen = seen.astype(jnp.bfloat16)
            for k in range(4):
                slot = lax.broadcasted_iota(jnp.int32, (128, 32), 0) // 8
                row = lax.broadcasted_iota(jnp.int32, (128, 32), 1)
                dy, dx = slot // 4, slot % 4
                block = lax.rem(zh + ORDER[k], 4) * 2 + ((x + dx) % 4) // 2
                put = (row == dy * 8 + block).astype(jnp.bfloat16)
                Mx[k, p, :, :, pl.ds(cc * items, items)] = dot(put, seen, NN).reshape(
                    16, 8, items
                )
    item_s.wait_recv()

    lanes = (slice(0, 128), slice(128, 256))

    def code(v, q_ref, f_ref):
        shape = v.shape
        v = v.reshape(-1, 8, 2 * 128)
        big = jnp.max(jnp.abs(v), axis=0)
        big = jnp.maximum(jnp.maximum(big[:, :128], big[:, 128:]), 1e-30)
        f_ref[...] = big * (1.0 / 32767.0)
        up = 32767.0 / big
        for l in lanes:
            q = jnp.round(v[:, :, l] * up).astype(jnp.int32).astype(jnp.int16)
            q_ref[..., l] = q.reshape(*shape[:-1], 128)

    def plain(q_ref, f_ref, l):
        q = q_ref[..., l].astype(jnp.int32).astype(jnp.float32)
        return (q.reshape(-1, 8, 128) * f_ref[...]).reshape(q.shape)

    def out1(k):
        for n in range(2):
            for d in far:
                v = PU[k, :, d, h1] if n else PU[k, d, :, h0]
                at = (k, n, d - 1)
                code(v, Q1.at[at], F1.at[at])
            start(back1[k][n])

    def sum1(k):
        for n in range(2):
            arrive(back1[k][n])
            own = PU[k, :, 0, h1] if n else PU[k, 0, :, h0]
            for l in lanes:
                v = own[..., l]
                for d in (1, 2, 3):
                    v += plain(R1.at[k, n, d - 1], E1.at[k, n, d - 1], l)
                S1[k, n, :, :, l] = v
            start(back2[k][n])

    def sum2(k):
        for n, h in ((0, h0), (1, h1)):
            arrive(back2[k][n])
            S2[k, h] = (S1[k, n, 0] + R2[k, 0, n]) + (R2[k, 1, n] + R2[k, 2, n])
        if k:
            back3[k - 1].start()

    tile = items // 2

    def step(i, carry):
        p = lax.div(i, 4)
        k = lax.rem(i + p, 4)
        for n in range(4):
            @pl.when(i == n)
            def _():
                arrive(second[n][0])
                arrive(second[n][1])

        @pl.when(i == 4)
        def _():
            item_f.wait_recv()

        w = G[k].reshape(16 * rows, 2 * width)

        def front(q):
            z = Z[2 * p + q // 2, pl.ds((q % 2) * tile, tile)]
            return z, dot(w[:, width:], z[:, :width], NT), dot(w, z, NT)

        def rear(q, z, s, t):
            e = jnp.exp(jnp.abs(s) * (-1.0 / 16.0))
            r = 1.0 / (1.0 + e)
            seen = Mx[k, p, :, :, pl.ds(q * tile, tile)]
            cu = (e * r * r * t).reshape(16, rows // 8, 8, tile) * seen[:, None]
            cu = cu.reshape(16 * rows, tile).astype(jnp.bfloat16)
            PV[2 * p + q // 2, pl.ds((q % 2) * tile, tile)] += dot(cu, w[:, width:], TN)
            return dot(cu, z[:, :width], NN)

        total, held = None, front(0)
        for q in range(4):
            now = held
            if q < 3:
                held = front(q + 1)
            part = rear(q, *now)
            total = part if total is None else total + part
        PU[k] += total.reshape(4, 4, rows, width)

        @pl.when(i == 2)
        def _():
            item_m.wait_recv()
            item_f.start()

        @pl.when(i == 3)
        def _():
            sum_s0.start()

        for n in range(4):
            @pl.when(i == 4 + n)
            def _():
                if n == 3:
                    sum_s1.start()
                out1((n + 1) % 4)

        return carry

    lax.fori_loop(0, 8, step, 0)
    sum_s1.wait_recv()
    code(PV[2] + RI1[1], QI, FI)
    start(sum_m)
    sum1(1)
    sum1(2)
    sum2(1)
    sum1(3)
    sum2(2)
    sum1(0)
    sum2(3)
    sum2(0)
    arrive(back3)
    out = 1.0 / 256.0
    ou[...] = ((S2[0] + R3[0]) + (R3[1] + R3[2])) * out
    sum_s0.wait_recv()
    arrive(sum_m)
    for l in lanes:
        oi[:, l] = (PV[0, :, l] + RI1[0, :, l] + plain(R4, E4, l)) * out
    for cp in made:
        cp.wait_send()


def on_device(user_factors, item_factors, user_tangent, item_tangent, block_mask):
    rows, width = user_factors.shape
    items = item_factors.shape[0]
    f32, bf16 = jnp.float32, jnp.bfloat16
    vmem = pl.BlockSpec(memory_space=pltpu.VMEM)
    scratch = [
        pltpu.VMEM((4, 4, 4, rows, 2 * width), bf16),
        pltpu.VMEM((4, items, 2 * width), bf16),
        pltpu.VMEM(block_mask.shape, jnp.int32),
        pltpu.VMEM((2, 4, 8, 128), f32),
        pltpu.VMEM((4, 2, 16, 8, 2 * items), f32),
        pltpu.VMEM((4, 4, 4, rows, width), f32),
        pltpu.VMEM((4, items, width), f32),
        pltpu.VMEM((4, 2, 3, 4, rows // 2, width), jnp.int16),
        pltpu.VMEM((4, 2, 3, 8, 128), f32),
        pltpu.VMEM((4, 2, 3, 4, rows // 2, width), jnp.int16),
        pltpu.VMEM((4, 2, 3, 8, 128), f32),
        pltpu.VMEM((4, 2, 4, rows // 2, width), f32),
        pltpu.VMEM((4, 3, 2, rows // 2, width), f32),
        pltpu.VMEM((4, rows, width), f32),
        pltpu.VMEM((3, rows, width), f32),
        pltpu.VMEM((2, items, width), f32),
        pltpu.VMEM((items, width), jnp.int16),
        pltpu.VMEM((8, 128), f32),
        pltpu.VMEM((items, width), jnp.int16),
        pltpu.VMEM((8, 128), f32),
        pltpu.SemaphoreType.DMA((N_SEM,)),
        pltpu.SemaphoreType.DMA((N_SEM,)),
        pltpu.SemaphoreType.DMA((5,)),
    ]
    args = (user_factors, user_tangent, item_factors, item_tangent, block_mask)
    hbm = [pltpu.with_memory_space_constraint(a, pltpu.HBM) for a in args]
    return pl.pallas_call(
        kernel,
        out_shape=(
            jax.ShapeDtypeStruct((rows, width), f32),
            jax.ShapeDtypeStruct((items, width), f32),
        ),
        in_specs=[pl.BlockSpec(memory_space=pltpu.HBM)] * 5,
        out_specs=[vmem] * 2,
        scratch_shapes=scratch,
        compiler_params=pltpu.CompilerParams(
            collective_id=0, has_side_effects=True, vmem_limit_bytes=40 << 20
        ),
    )(*hbm)


def solution(mesh):
    placed = (
        P(("au", "ia"), None),
        P(("ia", "au"), None),
        P(("au", "ia"), None),
        P(("ia", "au"), None),
        P("au", "ia"),
    )
    return jax.shard_map(
        on_device,
        mesh=mesh,
        in_specs=placed,
        out_specs=(P(("au", "ia"), None), P(("ia", "au"), None)),
        check_vma=False,
    )
```

```python
import jax
import jax.numpy as jnp
from jax import lax
from jax.experimental import pallas as pl
from jax.experimental.pallas import tpu as pltpu
from jax.sharding import PartitionSpec as P

MESH = pl.DeviceIdType.MESH
NT = (((1,), (1,)), ((), ()))
TN = (((0,), (0,)), ((), ()))
NN = (((1,), (0,)), ((), ()))
ORDER = (0, 1, 2, 3)
N_SEM = 56


def dot(a, b, dims):
    return lax.dot_general(a, b, dims, preferred_element_type=jnp.float32)


def kernel(
    uf, ut, vf, vt, mask, ou, oi,
    G, Z, mi, mb, Mx, PU, PV, Q1, F1, R1, E1, S1, R2, S2, R3, RI1, QI, FI, R4, E4, OU, OI, send, recv, local,
):
    au, ia = lax.axis_index("au"), lax.axis_index("ia")
    y, zl = lax.div(au, 2), lax.rem(au, 2)
    zh, x, c = lax.div(ia, 8), lax.rem(lax.div(ia, 2), 4), lax.rem(ia, 2)
    rows, width = uf.shape
    items = vf.shape[0]
    half = rows // 2

    def dev(dx=0, dy=0, dz=0, sib=False, mate=False):
        z = 1 - zl if mate else zl
        core = 1 - c if sib else c
        return (
            lax.rem(y + dy, 4) * 2 + z,
            (lax.rem(zh + dz, 4) * 4 + lax.rem(x + dx, 4)) * 2 + core,
        )

    partners = [dev(sib=True), dev(mate=True)]
    for d in (1, 2, 3):
        partners += [dev(dx=d), dev(dy=d), dev(dz=d)]
    barrier = pltpu.get_barrier_semaphore()
    for p in partners:
        pl.semaphore_signal(barrier, inc=1, device_id=p, device_id_type=MESH)

    left, right = pl.ds(0, width), pl.ds(width, width)
    place = [
        pltpu.make_async_copy(ut, G.at[0, 0, 0, :, left], local.at[0]),
        pltpu.make_async_copy(uf, G.at[0, 0, 0, :, right], local.at[1]),
        pltpu.make_async_copy(mask, mi, local.at[2]),
        pltpu.make_async_copy(vf, Z.at[0, :, left], local.at[3]),
        pltpu.make_async_copy(vt, Z.at[0, :, right], local.at[4]),
    ]
    for cp in place:
        cp.start()

    made = []

    class Set:
        def __init__(self, land, copies):
            n = len(made)
            made.append(self)

            def describe(src, dst, device):
                return pltpu.make_async_remote_copy(
                    src_ref=src,
                    dst_ref=dst,
                    send_sem=send.at[n],
                    recv_sem=recv.at[n],
                    device_id=device,
                    device_id_type=MESH,
                )

            self.copies = [describe(*cp) for cp in copies]
            self.all = describe(land, land, copies[0][2])

        def start(self):
            for cp in self.copies:
                cp.start()

        def wait_recv(self):
            self.all.wait_recv()

        def wait_send(self):
            self.all.wait_send()

    def copy(src, dst, device):
        return Set(dst, [(src, dst, device)])

    far = (1, 3, 2)
    h0, h1 = pl.ds(0, half), pl.ds(half, half)
    al, rest = pl.ds(0, 4), pl.ds(1, 3)
    by_z = {}
    for d in far:
        k = ORDER.index(4 - d)
        by_z[k] = copy(G.at[0, 0, 0], G.at[k, 0, 0], dev(dz=d))
    first, second = [], []
    for k in range(4):
        own = (G.at[k, 0, 0, h0], G.at[k, 0, 0, h1])
        first.append((
            Set(
                G.at[k, 0, rest, h0],
                [(own[0], G.at[k, 0, 4 - d, h0], dev(dx=d)) for d in far],
            ),
            Set(
                G.at[k, rest, 0, h1],
                [(own[1], G.at[k, 4 - d, 0, h1], dev(dy=d)) for d in far],
            ),
        ))
        own = (G.at[k, 0, al, h0], G.at[k, al, 0, h1])
        second.append((
            Set(
                G.at[k, rest, al, h0],
                [(own[0], G.at[k, 4 - d, al, h0], dev(dy=d)) for d in far],
            ),
            Set(
                G.at[k, al, rest, h1],
                [(own[1], G.at[k, al, 4 - d, h1], dev(dx=d)) for d in far],
            ),
        ))
    mask_y = Set(
        mb.at[0, rest], [(mb.at[0, 0], mb.at[0, 4 - d], dev(dy=d)) for d in far]
    )
    mask_c = copy(mb.at[0], mb.at[1], dev(sib=True))
    item_m = copy(Z.at[0], Z.at[2], dev(mate=True))
    item_s = copy(Z.at[0], Z.at[1], dev(sib=True))
    item_f = copy(Z.at[2], Z.at[3], dev(sib=True))
    gathers = list(made)
    back1, back2 = [], []
    for k in range(4):
        scales, sums, onward = [], [], []
        for n in range(2):
            to = [(d, dev(dx=d) if n else dev(dy=d)) for d in far]
            scales.append(
                Set(E1.at[k, n], [(F1.at[k, n, d - 1], E1.at[k, n, d - 1], t) for d, t in to])
            )
            sums.append(
                Set(R1.at[k, n], [(Q1.at[k, n, d - 1], R1.at[k, n, d - 1], t) for d, t in to])
            )
            to = [(d, dev(dy=d) if n else dev(dx=d)) for d in far]
            onward.append(
                Set(R2.at[k, n], [(S1.at[k, n, d], R2.at[k, n, d - 1], t) for d, t in to])
            )
        back1.append((scales, sums))
        back2.append(onward)
    back3 = Set(R3, [(S2.at[k], R3.at[k - 1], dev(dz=ORDER[k])) for k in (1, 2, 3)])
    sum_s0 = copy(PV.at[1], RI1.at[0], dev(sib=True))
    sum_s1 = copy(PV.at[3], RI1.at[1], dev(sib=True))
    quarter = items // 4
    sum_m = [copy(FI, E4, dev(mate=True))]
    for n in range(4):
        part = pl.ds(n * quarter, quarter)
        sum_m.append(copy(QI.at[part], R4.at[part], dev(mate=True)))

    def arrive(sets):
        for st in sets:
            st.wait_recv()

    def begin(sets):
        for st in sets:
            st.start()

    def after(came, then):
        for n in range(2):
            came[n].wait_recv()
            then[n].start()

    place[0].wait()
    place[1].wait()
    pl.semaphore_wait(barrier, len(partners))
    begin([by_z[1], by_z[3], by_z[2]])
    begin(first[0])
    place[3].wait()
    place[4].wait()
    item_m.start()
    item_s.start()
    place[2].wait()
    mb[0, 0] = jnp.zeros(mb.shape[2:], jnp.float32)
    mb[0, 0, :, : mask.shape[1]] = mi[...].astype(jnp.float32)
    mask_y.start()
    PU[...] = jnp.zeros_like(PU)
    PV[...] = jnp.zeros_like(PV)
    by_z[1].wait_recv()
    begin(first[1])
    by_z[3].wait_recv()
    begin(first[3])
    after(first[0], second[0])
    by_z[2].wait_recv()
    begin(first[2])
    mask_y.wait_recv()
    mask_c.start()

    def spread(p):
        zone = zl if p == 0 else 1 - zl
        j = lax.broadcasted_iota(jnp.int32, (128, items), 0)
        l = lax.broadcasted_iota(jnp.int32, (128, items), 1)
        pick = (j == 4 * (y * 2 + zone) + l // 128).astype(jnp.bfloat16)
        for cc in range(2):
            seen = dot(mb[cc].reshape(32, 128).astype(jnp.bfloat16), pick, NN)
            seen = seen.astype(jnp.bfloat16)
            for k in range(4):
                slot = lax.broadcasted_iota(jnp.int32, (128, 32), 0) // 8
                row = lax.broadcasted_iota(jnp.int32, (128, 32), 1)
                dy, dx = slot // 4, slot % 4
                block = lax.rem(zh + ORDER[k], 4) * 2 + ((x + dx) % 4) // 2
                put = (row == dy * 8 + block).astype(jnp.bfloat16)
                Mx[k, p, :, :, pl.ds(cc * items, items)] = dot(put, seen, NN).reshape(
                    16, 8, items
                )

    mask_c.wait_recv()
    spread(0)
    after(first[1], second[1])
    after(first[3], second[3])
    spread(1)
    after(first[2], second[2])
    item_s.wait_recv()

    lanes = (slice(0, 128), slice(128, 256))

    def code(v, q_ref, f_ref):
        shape = v.shape
        v = v.reshape(-1, 8, 2 * 128)
        big = jnp.max(jnp.abs(v), axis=0)
        big = jnp.maximum(jnp.maximum(big[:, :128], big[:, 128:]), 1e-30)
        f_ref[...] = big * (1.0 / 32767.0)
        up = 32767.0 / big
        for l in lanes:
            q = jnp.round(v[:, :, l] * up).astype(jnp.int32).astype(jnp.int16)
            q_ref[..., l] = q.reshape(*shape[:-1], 128)

    def plain(q_ref, f_ref, l):
        q = q_ref[..., l].astype(jnp.int32).astype(jnp.float32)
        return (q.reshape(-1, 8, 128) * f_ref[...]).reshape(q.shape)

    def out1(k):
        for n in range(2):
            for d in far:
                v = PU[k, :, d, h1] if n else PU[k, d, :, h0]
                at = (k, n, d - 1)
                code(v, Q1.at[at], F1.at[at])
            back1[k][0][n].start()
            back1[k][1][n].start()

    def sum1(k):
        for n in range(2):
            back1[k][0][n].wait_recv()
            back1[k][1][n].wait_recv()
            own = PU[k, :, 0, h1] if n else PU[k, 0, :, h0]
            for l in lanes:
                v = own[..., l]
                for d in (1, 2, 3):
                    v += plain(R1.at[k, n, d - 1], E1.at[k, n, d - 1], l)
                S1[k, n, :, :, l] = v
            back2[k][n].start()

    def sum2(k):
        for n, h in ((0, h0), (1, h1)):
            back2[k][n].wait_recv()
            S2[k, h] = (S1[k, n, 0] + R2[k, n, 0]) + (R2[k, n, 1] + R2[k, n, 2])
        if k:
            back3.copies[k - 1].start()

    tile = items // 2

    def step(i, carry):
        mid, late, last = lax.div(i + 6, 8), lax.div(i + 3, 8), lax.div(i, 7)
        p = mid - late + last
        k = i - mid - 2 * late - 4 * last

        for n in range(4):
            @pl.when(i == (0, 1, 3, 4)[n])
            def _():
                arrive(second[n])

        @pl.when(i == 1)
        def _():
            item_m.wait_recv()
            item_f.start()

        @pl.when(i == 2)
        def _():
            item_f.wait_recv()

        w = G[k].reshape(16 * rows, 2 * width)

        def front(q):
            z = Z[2 * p + q // 2, pl.ds((q % 2) * tile, tile)]
            return z, dot(w[:, width:], z[:, :width], NT), dot(w, z, NT)

        def rear(q, z, s, t):
            e = jnp.exp(jnp.abs(s) * (-1.0 / 16.0))
            r = 1.0 / (1.0 + e)
            seen = Mx[k, p, :, :, pl.ds(q * tile, tile)]
            cu = (e * r * r * t).reshape(16, rows // 8, 8, tile) * seen[:, None]
            cu = cu.reshape(16 * rows, tile).astype(jnp.bfloat16)
            PV[2 * p + q // 2, pl.ds((q % 2) * tile, tile)] += dot(cu, w[:, width:], TN)
            return dot(cu, z[:, :width], NN)

        total, held = None, front(0)
        for q in range(4):
            now = held
            if q < 3:
                held = front(q + 1)
            part = rear(q, *now)
            total = part if total is None else total + part
        PU[k] += total.reshape(4, 4, rows, width)

        for n in range(4):
            @pl.when(i == (7, 2, 5, 6)[n])
            def _():
                if n == 0:
                    sum_s1.start()
                out1(n)

        @pl.when(i == 5)
        def _():
            sum1(1)

        @pl.when(i == 6)
        def _():
            sum_s0.start()

        return carry

    lax.fori_loop(0, 8, step, 0)
    sum2(1)
    sum1(2)
    sum_s1.wait_recv()
    code(PV[2] + RI1[1], QI, FI)
    begin(sum_m[:3])
    sum1(3)
    sum_m[3].start()
    sum2(2)
    sum_m[4].start()
    sum1(0)
    sum2(3)
    for cp in gathers:
        cp.wait_send()
    sum2(0)
    out = 1.0 / 256.0
    sum_s0.wait_recv()
    arrive(sum_m)
    for l in lanes:
        OI[:, l] = (PV[0, :, l] + RI1[0, :, l] + plain(R4, E4, l)) * out
    away = [
        pltpu.make_async_copy(OU, ou, local.at[0]),
        pltpu.make_async_copy(OI, oi, local.at[1]),
    ]
    away[1].start()
    back3.wait_recv()
    OU[...] = ((S2[0] + R3[0]) + (R3[1] + R3[2])) * out
    away[0].start()
    for cp in made[len(gathers) :]:
        cp.wait_send()
    for cp in away:
        cp.wait()


def on_device(user_factors, item_factors, user_tangent, item_tangent, block_mask):
    rows, width = user_factors.shape
    items = item_factors.shape[0]
    f32, bf16 = jnp.float32, jnp.bfloat16
    scratch = [
        pltpu.VMEM((4, 4, 4, rows, 2 * width), bf16),
        pltpu.VMEM((4, items, 2 * width), bf16),
        pltpu.VMEM(block_mask.shape, jnp.int32),
        pltpu.VMEM((2, 4, 8, 128), f32),
        pltpu.VMEM((4, 2, 16, 8, 2 * items), f32),
        pltpu.VMEM((4, 4, 4, rows, width), f32),
        pltpu.VMEM((4, items, width), f32),
        pltpu.VMEM((4, 2, 3, 4, rows // 2, width), jnp.int16),
        pltpu.VMEM((4, 2, 3, 8, 128), f32),
        pltpu.VMEM((4, 2, 3, 4, rows // 2, width), jnp.int16),
        pltpu.VMEM((4, 2, 3, 8, 128), f32),
        pltpu.VMEM((4, 2, 4, rows // 2, width), f32),
        pltpu.VMEM((4, 2, 3, rows // 2, width), f32),
        pltpu.VMEM((4, rows, width), f32),
        pltpu.VMEM((3, rows, width), f32),
        pltpu.VMEM((2, items, width), f32),
        pltpu.VMEM((items, width), jnp.int16),
        pltpu.VMEM((8, 128), f32),
        pltpu.VMEM((items, width), jnp.int16),
        pltpu.VMEM((8, 128), f32),
        pltpu.VMEM((rows, width), f32),
        pltpu.VMEM((items, width), f32),
        pltpu.SemaphoreType.DMA((N_SEM,)),
        pltpu.SemaphoreType.DMA((N_SEM,)),
        pltpu.SemaphoreType.DMA((5,)),
    ]
    args = (user_factors, user_tangent, item_factors, item_tangent, block_mask)
    hbm = [pltpu.with_memory_space_constraint(a, pltpu.HBM) for a in args]
    return pl.pallas_call(
        kernel,
        out_shape=(
            jax.ShapeDtypeStruct((rows, width), f32),
            jax.ShapeDtypeStruct((items, width), f32),
        ),
        in_specs=[pl.BlockSpec(memory_space=pltpu.HBM)] * 5,
        out_specs=[pl.BlockSpec(memory_space=pl.ANY)] * 2,
        scratch_shapes=scratch,
        compiler_params=pltpu.CompilerParams(
            collective_id=0, has_side_effects=True, vmem_limit_bytes=40 << 20
        ),
    )(*hbm)


def solution(mesh):
    placed = (
        P(("au", "ia"), None),
        P(("ia", "au"), None),
        P(("au", "ia"), None),
        P(("ia", "au"), None),
        P("au", "ia"),
    )
    return jax.shard_map(
        on_device,
        mesh=mesh,
        in_specs=placed,
        out_specs=(P(("au", "ia"), None), P(("ia", "au"), None)),
        check_vma=False,
    )
```

```python
import jax
import jax.numpy as jnp
from jax import lax
from jax.experimental import pallas as pl
from jax.experimental.pallas import tpu as pltpu
from jax.sharding import PartitionSpec as P

MESH = pl.DeviceIdType.MESH
NT = (((1,), (1,)), ((), ()))
TN = (((0,), (0,)), ((), ()))
NN = (((1,), (0,)), ((), ()))
ORDER = (0, 1, 2, 3)
N_SEM = 57


def dot(a, b, dims):
    return lax.dot_general(a, b, dims, preferred_element_type=jnp.float32)


def kernel(
    uf, ut, vf, vt, mask, ou, oi,
    G, Z, mi, mb, Mx, PU, PV, Q1, F1, R1, E1, S1, R2, S2, Q3, F3, R3, E3, RI1, QI, FI, R4, E4, OU, OI, send, recv, local,
):
    au, ia = lax.axis_index("au"), lax.axis_index("ia")
    y, zl = lax.div(au, 2), lax.rem(au, 2)
    zh, x, c = lax.div(ia, 8), lax.rem(lax.div(ia, 2), 4), lax.rem(ia, 2)
    rows, width = uf.shape
    items = vf.shape[0]
    half = rows // 2

    def dev(dx=0, dy=0, dz=0, sib=False, mate=False):
        z = 1 - zl if mate else zl
        core = 1 - c if sib else c
        return (
            lax.rem(y + dy, 4) * 2 + z,
            (lax.rem(zh + dz, 4) * 4 + lax.rem(x + dx, 4)) * 2 + core,
        )

    partners = [dev(sib=True), dev(mate=True)]
    for d in (1, 2, 3):
        partners += [dev(dx=d), dev(dy=d), dev(dz=d)]
    barrier = pltpu.get_barrier_semaphore()
    for p in partners:
        pl.semaphore_signal(barrier, inc=1, device_id=p, device_id_type=MESH)

    left, right = pl.ds(0, width), pl.ds(width, width)
    place = [
        pltpu.make_async_copy(ut, G.at[0, 0, 0, :, left], local.at[0]),
        pltpu.make_async_copy(uf, G.at[0, 0, 0, :, right], local.at[1]),
        pltpu.make_async_copy(mask, mi, local.at[2]),
        pltpu.make_async_copy(vf, Z.at[0, :, left], local.at[3]),
        pltpu.make_async_copy(vt, Z.at[0, :, right], local.at[4]),
    ]
    for cp in place:
        cp.start()

    made = []

    class Set:
        def __init__(self, land, copies):
            n = len(made)
            made.append(self)

            def describe(src, dst, device):
                return pltpu.make_async_remote_copy(
                    src_ref=src,
                    dst_ref=dst,
                    send_sem=send.at[n],
                    recv_sem=recv.at[n],
                    device_id=device,
                    device_id_type=MESH,
                )

            self.copies = [describe(*cp) for cp in copies]
            self.all = describe(land, land, copies[0][2])

        def start(self):
            for cp in self.copies:
                cp.start()

        def wait_recv(self):
            self.all.wait_recv()

        def wait_send(self):
            self.all.wait_send()

    def copy(src, dst, device):
        return Set(dst, [(src, dst, device)])

    far = (1, 3, 2)
    h0, h1 = pl.ds(0, half), pl.ds(half, half)
    al, rest = pl.ds(0, 4), pl.ds(1, 3)
    by_z = {}
    for d in far:
        k = ORDER.index(4 - d)
        by_z[k] = copy(G.at[0, 0, 0], G.at[k, 0, 0], dev(dz=d))
    first, second = [], []
    for k in range(4):
        own = (G.at[k, 0, 0, h0], G.at[k, 0, 0, h1])
        first.append((
            Set(
                G.at[k, 0, rest, h0],
                [(own[0], G.at[k, 0, 4 - d, h0], dev(dx=d)) for d in far],
            ),
            Set(
                G.at[k, rest, 0, h1],
                [(own[1], G.at[k, 4 - d, 0, h1], dev(dy=d)) for d in far],
            ),
        ))
        own = (G.at[k, 0, al, h0], G.at[k, al, 0, h1])
        second.append((
            Set(
                G.at[k, rest, al, h0],
                [(own[0], G.at[k, 4 - d, al, h0], dev(dy=d)) for d in far],
            ),
            Set(
                G.at[k, al, rest, h1],
                [(own[1], G.at[k, al, 4 - d, h1], dev(dx=d)) for d in far],
            ),
        ))
    mask_y = Set(
        mb.at[0, rest], [(mb.at[0, 0], mb.at[0, 4 - d], dev(dy=d)) for d in far]
    )
    mask_c = copy(mb.at[0], mb.at[1], dev(sib=True))
    item_m = copy(Z.at[0], Z.at[2], dev(mate=True))
    item_s = copy(Z.at[0], Z.at[1], dev(sib=True))
    item_f = copy(Z.at[2], Z.at[3], dev(sib=True))
    gathers = list(made)
    back1, back2 = [], []
    for k in range(4):
        scales, sums, onward = [], [], []
        for n in range(2):
            to = [(d, dev(dx=d) if n else dev(dy=d)) for d in far]
            scales.append(
                Set(E1.at[k, n], [(F1.at[k, n, d - 1], E1.at[k, n, d - 1], t) for d, t in to])
            )
            sums.append(
                Set(R1.at[k, n], [(Q1.at[k, n, d - 1], R1.at[k, n, d - 1], t) for d, t in to])
            )
            to = [(d, dev(dy=d) if n else dev(dx=d)) for d in far]
            onward.append(
                Set(R2.at[k, n], [(S1.at[k, n, d], R2.at[k, n, d - 1], t) for d, t in to])
            )
        back1.append((scales, sums))
        back2.append(onward)
    to = [(k - 1, dev(dz=ORDER[k])) for k in (1, 2, 3)]
    back3 = [
        Set(E3, [(F3.at[n], E3.at[n], t) for n, t in to]),
        Set(R3, [(Q3.at[n], R3.at[n], t) for n, t in to]),
    ]
    sum_s0 = copy(PV.at[1], RI1.at[0], dev(sib=True))
    sum_s1 = copy(PV.at[3], RI1.at[1], dev(sib=True))
    quarter = items // 4
    sum_m = [copy(FI, E4, dev(mate=True))]
    for n in range(4):
        part = pl.ds(n * quarter, quarter)
        sum_m.append(copy(QI.at[part], R4.at[part], dev(mate=True)))

    def arrive(sets):
        for st in sets:
            st.wait_recv()

    def begin(sets):
        for st in sets:
            st.start()

    def after(came, then):
        for n in range(2):
            came[n].wait_recv()
            then[n].start()

    place[0].wait()
    place[1].wait()
    pl.semaphore_wait(barrier, len(partners))
    begin([by_z[1], by_z[3], by_z[2]])
    begin(first[0])
    place[3].wait()
    place[4].wait()
    item_m.start()
    item_s.start()
    place[2].wait()
    mb[0, 0] = jnp.zeros(mb.shape[2:], jnp.float32)
    mb[0, 0, :, : mask.shape[1]] = mi[...].astype(jnp.float32)
    mask_y.start()
    PU[...] = jnp.zeros_like(PU)
    PV[...] = jnp.zeros_like(PV)
    by_z[1].wait_recv()
    begin(first[1])
    by_z[3].wait_recv()
    begin(first[3])
    after(first[0], second[0])
    by_z[2].wait_recv()
    begin(first[2])
    mask_y.wait_recv()
    mask_c.start()

    def spread(p):
        zone = zl if p == 0 else 1 - zl
        j = lax.broadcasted_iota(jnp.int32, (128, items), 0)
        l = lax.broadcasted_iota(jnp.int32, (128, items), 1)
        pick = (j == 4 * (y * 2 + zone) + l // 128).astype(jnp.bfloat16)
        for cc in range(2):
            seen = dot(mb[cc].reshape(32, 128).astype(jnp.bfloat16), pick, NN)
            seen = seen.astype(jnp.bfloat16)
            for k in range(4):
                slot = lax.broadcasted_iota(jnp.int32, (128, 32), 0) // 8
                row = lax.broadcasted_iota(jnp.int32, (128, 32), 1)
                dy, dx = slot // 4, slot % 4
                block = lax.rem(zh + ORDER[k], 4) * 2 + ((x + dx) % 4) // 2
                put = (row == dy * 8 + block).astype(jnp.bfloat16)
                Mx[k, p, :, :, pl.ds(cc * items, items)] = dot(put, seen, NN).reshape(
                    16, 8, items
                )

    mask_c.wait_recv()
    spread(0)
    after(first[1], second[1])
    after(first[3], second[3])
    spread(1)
    after(first[2], second[2])
    item_s.wait_recv()

    lanes = (slice(0, 128), slice(128, 256))

    def code(v, q_ref, f_ref):
        shape = v.shape
        v = v.reshape(-1, 8, 2 * 128)
        big = jnp.max(jnp.abs(v), axis=0)
        big = jnp.maximum(jnp.maximum(big[:, :128], big[:, 128:]), 1e-30)
        f_ref[...] = big * (1.0 / 32767.0)
        up = 32767.0 / big
        for l in lanes:
            q = jnp.round(v[:, :, l] * up).astype(jnp.int32).astype(jnp.int16)
            q_ref[..., l] = q.reshape(*shape[:-1], 128)

    def plain(q_ref, f_ref, l):
        q = q_ref[..., l].astype(jnp.int32).astype(jnp.float32)
        return (q.reshape(-1, 8, 128) * f_ref[...]).reshape(q.shape)

    def out1(k):
        for n in range(2):
            for d in far:
                v = PU[k, :, d, h1] if n else PU[k, d, :, h0]
                at = (k, n, d - 1)
                code(v, Q1.at[at], F1.at[at])
            back1[k][0][n].start()
            back1[k][1][n].start()

    def sum1(k):
        for n in range(2):
            back1[k][0][n].wait_recv()
            back1[k][1][n].wait_recv()
            own = PU[k, :, 0, h1] if n else PU[k, 0, :, h0]
            for l in lanes:
                v = own[..., l]
                for d in (1, 2, 3):
                    v += plain(R1.at[k, n, d - 1], E1.at[k, n, d - 1], l)
                S1[k, n, :, :, l] = v
            back2[k][n].start()

    def sum2(k):
        for n, h in ((0, h0), (1, h1)):
            back2[k][n].wait_recv()
            S2[k, h] = (S1[k, n, 0] + R2[k, n, 0]) + (R2[k, n, 1] + R2[k, n, 2])
        if k:
            code(S2[k], Q3.at[k - 1], F3.at[k - 1])
            back3[0].copies[k - 1].start()
            back3[1].copies[k - 1].start()

    tile = items // 2

    def work(k, p):
        w = G[k].reshape(16 * rows, 2 * width)
        tiles = 8 if p is None else 4

        def at(q):
            return (q // 2 if p is None else 2 * p + q // 2), pl.ds((q % 2) * tile, tile)

        def front(q):
            z = Z[at(q)]
            return z, dot(w[:, width:], z[:, :width], NT), dot(w, z, NT)

        def rear(q, z, s, t):
            e = jnp.exp(jnp.abs(s) * (-1.0 / 16.0))
            r = 1.0 / (1.0 + e)
            side = q // 4 if p is None else p
            seen = Mx[k, side, :, :, pl.ds((q % 4) * tile, tile)]
            cu = (e * r * r * t).reshape(16, rows // 8, 8, tile) * seen[:, None]
            cu = cu.reshape(16 * rows, tile).astype(jnp.bfloat16)
            PV[at(q)] += dot(cu, w[:, width:], TN)
            return dot(cu, z[:, :width], NN)

        total, held = None, front(0)
        for q in range(tiles):
            now = held
            if q < tiles - 1:
                held = front(q + 1)
            part = rear(q, *now)
            total = part if total is None else total + part
        PU[k] += total.reshape(4, 4, rows, width)

    def early(i, carry):
        for n in range(2):
            @pl.when(i == n)
            def _():
                arrive(second[n])

        @pl.when(i == 1)
        def _():
            item_m.wait_recv()
            item_f.start()

        @pl.when(i == 2)
        def _():
            item_f.wait_recv()

        work(lax.div(i + 1, 2), lax.div(i, 2))
        return carry

    def late(k, carry):
        for n in (2, 3):
            @pl.when(k == n)
            def _():
                arrive(second[n])

        work(k, None)
        for n in (2, 3):
            @pl.when(k == n)
            def _():
                out1(n)
        return carry

    lax.fori_loop(0, 3, early, 0)
    out1(1)
    lax.fori_loop(2, 4, late, 0)
    sum1(1)
    sum_s0.start()
    work(0, 1)
    sum_s1.start()
    out1(0)
    sum1(2)
    sum_s1.wait_recv()
    code(PV[2] + RI1[1], QI, FI)
    begin(sum_m[:3])
    sum2(1)
    sum1(3)
    sum_m[3].start()
    sum2(2)
    sum_m[4].start()
    sum1(0)
    sum2(3)
    for cp in gathers:
        cp.wait_send()
    sum2(0)
    out = 1.0 / 256.0
    sum_s0.wait_recv()
    arrive(sum_m)
    for l in lanes:
        OI[:, l] = (PV[0, :, l] + RI1[0, :, l] + plain(R4, E4, l)) * out
    away = [
        pltpu.make_async_copy(OU, ou, local.at[0]),
        pltpu.make_async_copy(OI, oi, local.at[1]),
    ]
    away[1].start()
    arrive(back3)
    for l in lanes:
        v = S2[0, :, l]
        for n in range(3):
            v += plain(R3.at[n], E3.at[n], l)
        OU[:, l] = v * out
    away[0].start()
    for cp in made[len(gathers) :]:
        cp.wait_send()
    for cp in away:
        cp.wait()


def on_device(user_factors, item_factors, user_tangent, item_tangent, block_mask):
    rows, width = user_factors.shape
    items = item_factors.shape[0]
    f32, bf16 = jnp.float32, jnp.bfloat16
    scratch = [
        pltpu.VMEM((4, 4, 4, rows, 2 * width), bf16),
        pltpu.VMEM((4, items, 2 * width), bf16),
        pltpu.VMEM(block_mask.shape, jnp.int32),
        pltpu.VMEM((2, 4, 8, 128), f32),
        pltpu.VMEM((4, 2, 16, 8, 2 * items), f32),
        pltpu.VMEM((4, 4, 4, rows, width), f32),
        pltpu.VMEM((4, items, width), f32),
        pltpu.VMEM((4, 2, 3, 4, rows // 2, width), jnp.int16),
        pltpu.VMEM((4, 2, 3, 8, 128), f32),
        pltpu.VMEM((4, 2, 3, 4, rows // 2, width), jnp.int16),
        pltpu.VMEM((4, 2, 3, 8, 128), f32),
        pltpu.VMEM((4, 2, 4, rows // 2, width), f32),
        pltpu.VMEM((4, 2, 3, rows // 2, width), f32),
        pltpu.VMEM((4, rows, width), f32),
        pltpu.VMEM((3, rows, width), jnp.int16),
        pltpu.VMEM((3, 8, 128), f32),
        pltpu.VMEM((3, rows, width), jnp.int16),
        pltpu.VMEM((3, 8, 128), f32),
        pltpu.VMEM((2, items, width), f32),
        pltpu.VMEM((items, width), jnp.int16),
        pltpu.VMEM((8, 128), f32),
        pltpu.VMEM((items, width), jnp.int16),
        pltpu.VMEM((8, 128), f32),
        pltpu.VMEM((rows, width), f32),
        pltpu.VMEM((items, width), f32),
        pltpu.SemaphoreType.DMA((N_SEM,)),
        pltpu.SemaphoreType.DMA((N_SEM,)),
        pltpu.SemaphoreType.DMA((5,)),
    ]
    args = (user_factors, user_tangent, item_factors, item_tangent, block_mask)
    hbm = [pltpu.with_memory_space_constraint(a, pltpu.HBM) for a in args]
    return pl.pallas_call(
        kernel,
        out_shape=(
            jax.ShapeDtypeStruct((rows, width), f32),
            jax.ShapeDtypeStruct((items, width), f32),
        ),
        in_specs=[pl.BlockSpec(memory_space=pltpu.HBM)] * 5,
        out_specs=[pl.BlockSpec(memory_space=pl.ANY)] * 2,
        scratch_shapes=scratch,
        compiler_params=pltpu.CompilerParams(
            collective_id=0, has_side_effects=True, vmem_limit_bytes=40 << 20
        ),
    )(*hbm)


def solution(mesh):
    placed = (
        P(("au", "ia"), None),
        P(("ia", "au"), None),
        P(("au", "ia"), None),
        P(("ia", "au"), None),
        P("au", "ia"),
    )
    return jax.shard_map(
        on_device,
        mesh=mesh,
        in_specs=placed,
        out_specs=(P(("au", "ia"), None), P(("ia", "au"), None)),
        check_vma=False,
    )
```

```python
import jax
import jax.numpy as jnp
from jax import lax
from jax.experimental import pallas as pl
from jax.experimental.pallas import tpu as pltpu
from jax.sharding import PartitionSpec as P

MESH = pl.DeviceIdType.MESH
NT = (((1,), (1,)), ((), ()))
TN = (((0,), (0,)), ((), ()))
NN = (((1,), (0,)), ((), ()))
ORDER = (0, 1, 2, 3)
N_SEM = 59


def dot(a, b, dims):
    return lax.dot_general(a, b, dims, preferred_element_type=jnp.float32)


def kernel(
    uf, ut, vf, vt, mask, ou, oi,
    G, Z, mi, mb, Mx, PU, PV, Q1, F1, R1, E1, S1, R2, S2, Q3, F3, R3, E3, RI1, QI, FI, R4, E4, OU, OI, send, recv, local,
):
    au, ia = lax.axis_index("au"), lax.axis_index("ia")
    y, zl = lax.div(au, 2), lax.rem(au, 2)
    zh, x, c = lax.div(ia, 8), lax.rem(lax.div(ia, 2), 4), lax.rem(ia, 2)
    rows, width = uf.shape
    items = vf.shape[0]
    half = rows // 2

    def dev(dx=0, dy=0, dz=0, sib=False, mate=False):
        z = 1 - zl if mate else zl
        core = 1 - c if sib else c
        return (
            lax.rem(y + dy, 4) * 2 + z,
            (lax.rem(zh + dz, 4) * 4 + lax.rem(x + dx, 4)) * 2 + core,
        )

    partners = [dev(sib=True), dev(mate=True)]
    for d in (1, 2, 3):
        partners += [dev(dx=d), dev(dy=d), dev(dz=d)]
    barrier = pltpu.get_barrier_semaphore()
    for p in partners:
        pl.semaphore_signal(barrier, inc=1, device_id=p, device_id_type=MESH)

    left, right = pl.ds(0, width), pl.ds(width, width)
    place = [
        pltpu.make_async_copy(ut, G.at[0, 0, 0, :, left], local.at[0]),
        pltpu.make_async_copy(uf, G.at[0, 0, 0, :, right], local.at[1]),
        pltpu.make_async_copy(mask, mi, local.at[2]),
        pltpu.make_async_copy(vf, Z.at[0, :, left], local.at[3]),
        pltpu.make_async_copy(vt, Z.at[0, :, right], local.at[4]),
    ]
    for cp in place:
        cp.start()

    made = []

    class Set:
        def __init__(self, land, copies):
            n = len(made)
            made.append(self)

            def describe(src, dst, device):
                return pltpu.make_async_remote_copy(
                    src_ref=src,
                    dst_ref=dst,
                    send_sem=send.at[n],
                    recv_sem=recv.at[n],
                    device_id=device,
                    device_id_type=MESH,
                )

            self.copies = [describe(*cp) for cp in copies]
            self.all = describe(land, land, copies[0][2])

        def start(self):
            for cp in self.copies:
                cp.start()

        def wait_recv(self):
            self.all.wait_recv()

        def wait_send(self):
            self.all.wait_send()

    def copy(src, dst, device):
        return Set(dst, [(src, dst, device)])

    far = (1, 3, 2)
    h0, h1 = pl.ds(0, half), pl.ds(half, half)
    al, rest = pl.ds(0, 4), pl.ds(1, 3)
    by_z = {}
    for d in far:
        k = ORDER.index(4 - d)
        by_z[k] = copy(G.at[0, 0, 0], G.at[k, 0, 0], dev(dz=d))
    first, second = [], []
    for k in range(4):
        own = (G.at[k, 0, 0, h0], G.at[k, 0, 0, h1])
        first.append((
            Set(
                G.at[k, 0, rest, h0],
                [(own[0], G.at[k, 0, 4 - d, h0], dev(dx=d)) for d in far],
            ),
            Set(
                G.at[k, rest, 0, h1],
                [(own[1], G.at[k, 4 - d, 0, h1], dev(dy=d)) for d in far],
            ),
        ))
        own = (G.at[k, 0, al, h0], G.at[k, al, 0, h1])
        second.append((
            Set(
                G.at[k, rest, al, h0],
                [(own[0], G.at[k, 4 - d, al, h0], dev(dy=d)) for d in far],
            ),
            Set(
                G.at[k, al, rest, h1],
                [(own[1], G.at[k, al, 4 - d, h1], dev(dx=d)) for d in far],
            ),
        ))
    mask_y = Set(
        mb.at[0, rest], [(mb.at[0, 0], mb.at[0, 4 - d], dev(dy=d)) for d in far]
    )
    mask_c = copy(mb.at[0], mb.at[1], dev(sib=True))
    h = (pl.ds(0, items // 2), pl.ds(items // 2, items // 2))
    item_m = [copy(Z.at[0, n], Z.at[2, n], dev(mate=True)) for n in h]
    item_s = copy(Z.at[0], Z.at[1], dev(sib=True))
    item_f = [copy(Z.at[2, n], Z.at[3, n], dev(sib=True)) for n in h]
    gathers = list(made)
    back1, back2 = [], []
    for k in range(4):
        scales, sums, onward = [], [], []
        for n in range(2):
            to = [(d, dev(dx=d) if n else dev(dy=d)) for d in far]
            scales.append(
                Set(E1.at[k, n], [(F1.at[k, n, d - 1], E1.at[k, n, d - 1], t) for d, t in to])
            )
            sums.append(
                Set(R1.at[k, n], [(Q1.at[k, n, d - 1], R1.at[k, n, d - 1], t) for d, t in to])
            )
            to = [(d, dev(dy=d) if n else dev(dx=d)) for d in far]
            onward.append(
                Set(R2.at[k, n], [(S1.at[k, n, d], R2.at[k, n, d - 1], t) for d, t in to])
            )
        back1.append((scales, sums))
        back2.append(onward)
    to = [(k - 1, dev(dz=ORDER[k])) for k in (1, 2, 3)]
    back3 = [
        Set(E3, [(F3.at[n], E3.at[n], t) for n, t in to]),
        Set(R3, [(Q3.at[n], R3.at[n], t) for n, t in to]),
    ]
    sum_s0 = copy(PV.at[1], RI1.at[0], dev(sib=True))
    sum_s1 = copy(PV.at[3], RI1.at[1], dev(sib=True))
    quarter = items // 4
    sum_m = [copy(FI, E4, dev(mate=True))]
    for n in range(4):
        part = pl.ds(n * quarter, quarter)
        sum_m.append(copy(QI.at[part], R4.at[part], dev(mate=True)))

    def arrive(sets):
        for st in sets:
            st.wait_recv()

    def begin(sets):
        for st in sets:
            st.start()

    def after(came, then):
        for n in range(2):
            came[n].wait_recv()
            then[n].start()

    place[0].wait()
    place[1].wait()
    pl.semaphore_wait(barrier, len(partners))
    begin([by_z[1], by_z[3], by_z[2]])
    begin(first[0])
    place[3].wait()
    place[4].wait()
    begin(item_m)
    item_s.start()
    place[2].wait()
    mb[0, 0] = jnp.zeros(mb.shape[2:], jnp.float32)
    mb[0, 0, :, : mask.shape[1]] = mi[...].astype(jnp.float32)
    mask_y.start()
    PU[...] = jnp.zeros_like(PU)
    PV[...] = jnp.zeros_like(PV)
    by_z[1].wait_recv()
    begin(first[1])
    by_z[3].wait_recv()
    begin(first[3])
    after(first[0], second[0])
    by_z[2].wait_recv()
    begin(first[2])
    mask_y.wait_recv()
    mask_c.start()

    def spread(p):
        zone = zl if p == 0 else 1 - zl
        j = lax.broadcasted_iota(jnp.int32, (128, items), 0)
        l = lax.broadcasted_iota(jnp.int32, (128, items), 1)
        pick = (j == 4 * (y * 2 + zone) + l // 128).astype(jnp.bfloat16)
        for cc in range(2):
            seen = dot(mb[cc].reshape(32, 128).astype(jnp.bfloat16), pick, NN)
            seen = seen.astype(jnp.bfloat16)
            for k in range(4):
                slot = lax.broadcasted_iota(jnp.int32, (128, 32), 0) // 8
                row = lax.broadcasted_iota(jnp.int32, (128, 32), 1)
                dy, dx = slot // 4, slot % 4
                block = lax.rem(zh + ORDER[k], 4) * 2 + ((x + dx) % 4) // 2
                put = (row == dy * 8 + block).astype(jnp.bfloat16)
                Mx[k, p, :, :, pl.ds(cc * items, items)] = dot(put, seen, NN).reshape(
                    16, 8, items
                )

    mask_c.wait_recv()
    spread(0)
    after(first[1], second[1])
    after(first[3], second[3])
    spread(1)
    after(first[2], second[2])
    item_s.wait_recv()

    lanes = (slice(0, 128), slice(128, 256))

    def code(v, q_ref, f_ref):
        shape = v.shape
        v = v.reshape(-1, 8, 2 * 128)
        big = jnp.max(jnp.abs(v), axis=0)
        big = jnp.maximum(jnp.maximum(big[:, :128], big[:, 128:]), 1e-30)
        f_ref[...] = big * (1.0 / 32767.0)
        up = 32767.0 / big
        for l in lanes:
            q = jnp.round(v[:, :, l] * up).astype(jnp.int32).astype(jnp.int16)
            q_ref[..., l] = q.reshape(*shape[:-1], 128)

    def plain(q_ref, f_ref, l):
        q = q_ref[..., l].astype(jnp.int32).astype(jnp.float32)
        return (q.reshape(-1, 8, 128) * f_ref[...]).reshape(q.shape)

    def out1(k):
        for n in range(2):
            for d in far:
                v = PU[k, :, d, h1] if n else PU[k, d, :, h0]
                at = (k, n, d - 1)
                code(v, Q1.at[at], F1.at[at])
            back1[k][0][n].start()
            back1[k][1][n].start()

    def sum1(k):
        for n in range(2):
            back1[k][0][n].wait_recv()
            back1[k][1][n].wait_recv()
            own = PU[k, :, 0, h1] if n else PU[k, 0, :, h0]
            for l in lanes:
                v = own[..., l]
                for d in (1, 2, 3):
                    v += plain(R1.at[k, n, d - 1], E1.at[k, n, d - 1], l)
                S1[k, n, :, :, l] = v
            back2[k][n].start()

    def sum2(k):
        for n, h in ((0, h0), (1, h1)):
            back2[k][n].wait_recv()
            S2[k, h] = (S1[k, n, 0] + R2[k, n, 0]) + (R2[k, n, 1] + R2[k, n, 2])
        if k:
            code(S2[k], Q3.at[k - 1], F3.at[k - 1])
            back3[0].copies[k - 1].start()
            back3[1].copies[k - 1].start()

    tile = items // 2

    def work(k, tiles):
        w = G[k].reshape(16 * rows, 2 * width)

        def at(q):
            side, core, n = tiles[q]
            return 2 * side + core, pl.ds(n * tile, tile)

        def front(q):
            z = Z[at(q)]
            return z, dot(w[:, width:], z[:, :width], NT), dot(w, z, NT)

        def rear(q, z, s, t):
            e = jnp.exp(jnp.abs(s) * (-1.0 / 16.0))
            r = 1.0 / (1.0 + e)
            side, core, n = tiles[q]
            seen = Mx[k, side, :, :, pl.ds((2 * core + n) * tile, tile)]
            cu = (e * r * r * t).reshape(16, rows // 8, 8, tile) * seen[:, None]
            cu = cu.reshape(16 * rows, tile).astype(jnp.bfloat16)
            PV[at(q)] += dot(cu, w[:, width:], TN)
            return dot(cu, z[:, :width], NN)

        total, held = None, front(0)
        for q in range(len(tiles)):
            now = held
            if q < len(tiles) - 1:
                held = front(q + 1)
            part = rear(q, *now)
            total = part if total is None else total + part
        PU[k] += total.reshape(4, 4, rows, width)

    halves = [(core, n) for core in range(2) for n in range(2)]

    def early(i, carry):
        @pl.when(i == 0)
        def _():
            arrive(second[0])

        @pl.when(i == 1)
        def _():
            item_f[0].wait_recv()
            work(0, [(1, 0, 0), (1, 1, 0)])
            arrive(second[1])
            item_m[1].wait_recv()
            item_f[1].start()

        @pl.when(i == 2)
        def _():
            item_f[1].wait_recv()

        work(lax.div(i + 1, 2), [(lax.div(i, 2), *ch) for ch in halves])
        return carry

    def late(k, carry):
        for n in (2, 3):
            @pl.when(k == n)
            def _():
                arrive(second[n])

        work(k, [(side, *ch) for side in range(2) for ch in halves])
        for n in (2, 3):
            @pl.when(k == n)
            def _():
                out1(n)
        return carry

    item_m[0].wait_recv()
    item_f[0].start()
    lax.fori_loop(0, 3, early, 0)
    out1(1)
    lax.fori_loop(2, 4, late, 0)
    sum1(1)
    sum_s0.start()
    work(0, [(1, 1, 1), (1, 0, 1)])
    sum_s1.start()
    out1(0)
    sum1(2)
    sum_s1.wait_recv()
    code(PV[2] + RI1[1], QI, FI)
    begin(sum_m[:3])
    sum2(1)
    sum1(3)
    sum_m[3].start()
    sum2(2)
    sum_m[4].start()
    sum1(0)
    sum2(3)
    for cp in gathers:
        cp.wait_send()
    sum2(0)
    out = 1.0 / 256.0
    sum_s0.wait_recv()
    arrive(sum_m)
    for l in lanes:
        OI[:, l] = (PV[0, :, l] + RI1[0, :, l] + plain(R4, E4, l)) * out
    away = [
        pltpu.make_async_copy(OU, ou, local.at[0]),
        pltpu.make_async_copy(OI, oi, local.at[1]),
    ]
    away[1].start()
    arrive(back3)
    for l in lanes:
        v = S2[0, :, l]
        for n in range(3):
            v += plain(R3.at[n], E3.at[n], l)
        OU[:, l] = v * out
    away[0].start()
    for cp in made[len(gathers) :]:
        cp.wait_send()
    for cp in away:
        cp.wait()


def on_device(user_factors, item_factors, user_tangent, item_tangent, block_mask):
    rows, width = user_factors.shape
    items = item_factors.shape[0]
    f32, bf16 = jnp.float32, jnp.bfloat16
    scratch = [
        pltpu.VMEM((4, 4, 4, rows, 2 * width), bf16),
        pltpu.VMEM((4, items, 2 * width), bf16),
        pltpu.VMEM(block_mask.shape, jnp.int32),
        pltpu.VMEM((2, 4, 8, 128), f32),
        pltpu.VMEM((4, 2, 16, 8, 2 * items), f32),
        pltpu.VMEM((4, 4, 4, rows, width), f32),
        pltpu.VMEM((4, items, width), f32),
        pltpu.VMEM((4, 2, 3, 4, rows // 2, width), jnp.int16),
        pltpu.VMEM((4, 2, 3, 8, 128), f32),
        pltpu.VMEM((4, 2, 3, 4, rows // 2, width), jnp.int16),
        pltpu.VMEM((4, 2, 3, 8, 128), f32),
        pltpu.VMEM((4, 2, 4, rows // 2, width), f32),
        pltpu.VMEM((4, 2, 3, rows // 2, width), f32),
        pltpu.VMEM((4, rows, width), f32),
        pltpu.VMEM((3, rows, width), jnp.int16),
        pltpu.VMEM((3, 8, 128), f32),
        pltpu.VMEM((3, rows, width), jnp.int16),
        pltpu.VMEM((3, 8, 128), f32),
        pltpu.VMEM((2, items, width), f32),
        pltpu.VMEM((items, width), jnp.int16),
        pltpu.VMEM((8, 128), f32),
        pltpu.VMEM((items, width), jnp.int16),
        pltpu.VMEM((8, 128), f32),
        pltpu.VMEM((rows, width), f32),
        pltpu.VMEM((items, width), f32),
        pltpu.SemaphoreType.DMA((N_SEM,)),
        pltpu.SemaphoreType.DMA((N_SEM,)),
        pltpu.SemaphoreType.DMA((5,)),
    ]
    args = (user_factors, user_tangent, item_factors, item_tangent, block_mask)
    hbm = [pltpu.with_memory_space_constraint(a, pltpu.HBM) for a in args]
    return pl.pallas_call(
        kernel,
        out_shape=(
            jax.ShapeDtypeStruct((rows, width), f32),
            jax.ShapeDtypeStruct((items, width), f32),
        ),
        in_specs=[pl.BlockSpec(memory_space=pltpu.HBM)] * 5,
        out_specs=[pl.BlockSpec(memory_space=pl.ANY)] * 2,
        scratch_shapes=scratch,
        compiler_params=pltpu.CompilerParams(
            collective_id=0, has_side_effects=True, vmem_limit_bytes=40 << 20
        ),
    )(*hbm)


def solution(mesh):
    placed = (
        P(("au", "ia"), None),
        P(("ia", "au"), None),
        P(("au", "ia"), None),
        P(("ia", "au"), None),
        P("au", "ia"),
    )
    return jax.shard_map(
        on_device,
        mesh=mesh,
        in_specs=placed,
        out_specs=(P(("au", "ia"), None), P(("ia", "au"), None)),
        check_vma=False,
    )
```

```python
import jax
import jax.numpy as jnp
from jax import lax
from jax.experimental import pallas as pl
from jax.experimental.pallas import tpu as pltpu
from jax.sharding import PartitionSpec as P

MESH = pl.DeviceIdType.MESH
NT = (((1,), (1,)), ((), ()))
TN = (((0,), (0,)), ((), ()))
NN = (((1,), (0,)), ((), ()))
ORDER = (0, 1, 2, 3)
N_SEM = 59


def dot(a, b, dims):
    return lax.dot_general(a, b, dims, preferred_element_type=jnp.float32)


def kernel(
    uf, ut, vf, vt, mask, ou, oi,
    G, Z, mi, mb, Mx, PU, PV, Q1, F1, R1, E1, S1, R2, S2, Q3, F3, R3, E3, RI1, QI, FI, R4, E4, OU, OI, send, recv, local,
):
    au, ia = lax.axis_index("au"), lax.axis_index("ia")
    y, zl = lax.div(au, 2), lax.rem(au, 2)
    zh, x, c = lax.div(ia, 8), lax.rem(lax.div(ia, 2), 4), lax.rem(ia, 2)
    rows, width = uf.shape
    items = vf.shape[0]
    half = rows // 2

    def dev(dx=0, dy=0, dz=0, sib=False, mate=False):
        z = 1 - zl if mate else zl
        core = 1 - c if sib else c
        return (
            lax.rem(y + dy, 4) * 2 + z,
            (lax.rem(zh + dz, 4) * 4 + lax.rem(x + dx, 4)) * 2 + core,
        )

    partners = [dev(sib=True), dev(mate=True)]
    for d in (1, 2, 3):
        partners += [dev(dx=d), dev(dy=d), dev(dz=d)]
    barrier = pltpu.get_barrier_semaphore()
    for p in partners:
        pl.semaphore_signal(barrier, inc=1, device_id=p, device_id_type=MESH)

    left, right = pl.ds(0, width), pl.ds(width, width)
    place = [
        pltpu.make_async_copy(ut, G.at[0, 0, 0, :, left], local.at[0]),
        pltpu.make_async_copy(uf, G.at[0, 0, 0, :, right], local.at[1]),
        pltpu.make_async_copy(mask, mi, local.at[2]),
        pltpu.make_async_copy(vf, Z.at[0, :, left], local.at[3]),
        pltpu.make_async_copy(vt, Z.at[0, :, right], local.at[4]),
    ]
    for cp in place:
        cp.start()

    made = []

    class Set:
        def __init__(self, land, copies):
            n = len(made)
            made.append(self)

            def describe(src, dst, device):
                return pltpu.make_async_remote_copy(
                    src_ref=src,
                    dst_ref=dst,
                    send_sem=send.at[n],
                    recv_sem=recv.at[n],
                    device_id=device,
                    device_id_type=MESH,
                )

            self.copies = [describe(*cp) for cp in copies]
            self.all = describe(land, land, copies[0][2])

        def start(self):
            for cp in self.copies:
                cp.start()

        def wait_recv(self):
            self.all.wait_recv()

        def wait_send(self):
            self.all.wait_send()

    def copy(src, dst, device):
        return Set(dst, [(src, dst, device)])

    far = (1, 3, 2)
    h0, h1 = pl.ds(0, half), pl.ds(half, half)
    al, rest = pl.ds(0, 4), pl.ds(1, 3)
    by_z = {}
    for d in far:
        k = ORDER.index(4 - d)
        by_z[k] = copy(G.at[0, 0, 0], G.at[k, 0, 0], dev(dz=d))
    first, second = [], []
    for k in range(4):
        own = (G.at[k, 0, 0, h0], G.at[k, 0, 0, h1])
        first.append((
            Set(
                G.at[k, 0, rest, h0],
                [(own[0], G.at[k, 0, 4 - d, h0], dev(dx=d)) for d in far],
            ),
            Set(
                G.at[k, rest, 0, h1],
                [(own[1], G.at[k, 4 - d, 0, h1], dev(dy=d)) for d in far],
            ),
        ))
        own = (G.at[k, 0, al, h0], G.at[k, al, 0, h1])
        second.append((
            Set(
                G.at[k, rest, al, h0],
                [(own[0], G.at[k, 4 - d, al, h0], dev(dy=d)) for d in far],
            ),
            Set(
                G.at[k, al, rest, h1],
                [(own[1], G.at[k, al, 4 - d, h1], dev(dx=d)) for d in far],
            ),
        ))
    mask_y = Set(
        mb.at[0, rest], [(mb.at[0, 0], mb.at[0, 4 - d], dev(dy=d)) for d in far]
    )
    mask_c = copy(mb.at[0], mb.at[1], dev(sib=True))
    h = (pl.ds(0, items // 2), pl.ds(items // 2, items // 2))
    item_m = [copy(Z.at[0, n], Z.at[2, n], dev(mate=True)) for n in h]
    item_s = copy(Z.at[0], Z.at[1], dev(sib=True))
    item_f = [copy(Z.at[2, n], Z.at[3, n], dev(sib=True)) for n in h]
    gathers = list(made)
    back1, back2 = [], []
    for k in range(4):
        scales, sums, onward = [], [], []
        for n in range(2):
            to = [(d, dev(dx=d) if n else dev(dy=d)) for d in far]
            scales.append(
                Set(E1.at[k, n], [(F1.at[k, n, d - 1], E1.at[k, n, d - 1], t) for d, t in to])
            )
            sums.append(
                Set(R1.at[k, n], [(Q1.at[k, n, d - 1], R1.at[k, n, d - 1], t) for d, t in to])
            )
            to = [(d, dev(dy=d) if n else dev(dx=d)) for d in far]
            onward.append(
                Set(R2.at[k, n], [(S1.at[k, n, d], R2.at[k, n, d - 1], t) for d, t in to])
            )
        back1.append((scales, sums))
        back2.append(onward)
    to = [(k - 1, dev(dz=ORDER[k])) for k in (1, 2, 3)]
    back3 = [
        Set(E3, [(F3.at[n], E3.at[n], t) for n, t in to]),
        Set(R3, [(Q3.at[n], R3.at[n], t) for n, t in to]),
    ]
    sum_s0 = copy(PV.at[1], RI1.at[0], dev(sib=True))
    sum_s1 = copy(PV.at[3], RI1.at[1], dev(sib=True))
    quarter = items // 4
    sum_m = [copy(FI, E4, dev(mate=True))]
    for n in range(4):
        part = pl.ds(n * quarter, quarter)
        sum_m.append(copy(QI.at[part], R4.at[part], dev(mate=True)))

    def arrive(sets):
        for st in sets:
            st.wait_recv()

    def begin(sets):
        for st in sets:
            st.start()

    def after(came, then):
        for n in range(2):
            came[n].wait_recv()
            then[n].start()

    place[0].wait()
    place[1].wait()
    pl.semaphore_wait(barrier, len(partners))
    begin([by_z[1], by_z[3], by_z[2]])
    begin(first[0])
    place[3].wait()
    place[4].wait()
    begin(item_m)
    item_s.start()
    place[2].wait()
    mb[0, 0] = jnp.zeros(mb.shape[2:], jnp.float32)
    mb[0, 0, :, : mask.shape[1]] = mi[...].astype(jnp.float32)
    mask_y.start()
    PU[...] = jnp.zeros_like(PU)
    PV[...] = jnp.zeros_like(PV)
    by_z[1].wait_recv()
    begin(first[1])
    by_z[3].wait_recv()
    begin(first[3])
    after(first[0], second[0])
    by_z[2].wait_recv()
    begin(first[2])
    mask_y.wait_recv()
    mask_c.start()

    def spread(p):
        zone = zl if p == 0 else 1 - zl
        j = lax.broadcasted_iota(jnp.int32, (128, items), 0)
        l = lax.broadcasted_iota(jnp.int32, (128, items), 1)
        pick = (j == 4 * (y * 2 + zone) + l // 128).astype(jnp.bfloat16)
        for cc in range(2):
            seen = dot(mb[cc].reshape(32, 128).astype(jnp.bfloat16), pick, NN)
            seen = seen.astype(jnp.bfloat16)
            for k in range(4):
                slot = lax.broadcasted_iota(jnp.int32, (128, 32), 0) // 8
                row = lax.broadcasted_iota(jnp.int32, (128, 32), 1)
                dy, dx = slot // 4, slot % 4
                block = lax.rem(zh + ORDER[k], 4) * 2 + ((x + dx) % 4) // 2
                put = (row == dy * 8 + block).astype(jnp.bfloat16)
                Mx[k, p, :, :, pl.ds(cc * items, items)] = dot(put, seen, NN).reshape(
                    16, 8, items
                )

    mask_c.wait_recv()
    spread(0)
    after(first[1], second[1])
    after(first[3], second[3])
    spread(1)
    after(first[2], second[2])
    item_s.wait_recv()

    lanes = (slice(0, 128), slice(128, 256))

    def code(v, q_ref, f_ref):
        shape = v.shape
        v = v.reshape(-1, 8, 2 * 128)
        big = jnp.max(jnp.abs(v), axis=0)
        big = jnp.maximum(jnp.maximum(big[:, :128], big[:, 128:]), 1e-30)
        f_ref[...] = big * (1.0 / 32767.0)
        up = 32767.0 / big
        for l in lanes:
            q = jnp.round(v[:, :, l] * up).astype(jnp.int32).astype(jnp.int16)
            q_ref[..., l] = q.reshape(*shape[:-1], 128)

    def plain(q_ref, f_ref, l):
        q = q_ref[..., l].astype(jnp.int32).astype(jnp.float32)
        return (q.reshape(-1, 8, 128) * f_ref[...]).reshape(q.shape)

    def out1(k):
        for n in range(2):
            for d in far:
                v = PU[k, :, d, h1] if n else PU[k, d, :, h0]
                at = (k, n, d - 1)
                code(v, Q1.at[at], F1.at[at])
            back1[k][0][n].start()
            back1[k][1][n].start()

    def sum1(k):
        for n in range(2):
            back1[k][0][n].wait_recv()
            back1[k][1][n].wait_recv()
            own = PU[k, :, 0, h1] if n else PU[k, 0, :, h0]
            for l in lanes:
                v = own[..., l]
                for d in (1, 2, 3):
                    v += plain(R1.at[k, n, d - 1], E1.at[k, n, d - 1], l)
                S1[k, n, :, :, l] = v
            back2[k][n].start()

    def sum2(k):
        for n, h in ((0, h0), (1, h1)):
            back2[k][n].wait_recv()
            S2[k, h] = (S1[k, n, 0] + R2[k, n, 0]) + (R2[k, n, 1] + R2[k, n, 2])
        if k:
            code(S2[k], Q3.at[k - 1], F3.at[k - 1])
            back3[0].copies[k - 1].start()
            back3[1].copies[k - 1].start()

    tile = items // 2

    def work(k, tiles):
        w = G[k].reshape(16 * rows, 2 * width)

        def at(q):
            side, core, n = tiles[q]
            return 2 * side + core, pl.ds(n * tile, tile)

        def front(q):
            z = Z[at(q)]
            return z, dot(w[:, width:], z[:, :width], NT), dot(w, z, NT)

        def rear(q, z, s, t):
            e = jnp.exp(jnp.abs(s) * (-1.0 / 16.0))
            r = 1.0 / (1.0 + e)
            side, core, n = tiles[q]
            seen = Mx[k, side, :, :, pl.ds((2 * core + n) * tile, tile)]
            cu = (e * r * r * t).reshape(16, rows // 8, 8, tile) * seen[:, None]
            cu = cu.reshape(16 * rows, tile).astype(jnp.bfloat16)
            PV[at(q)] += dot(cu, w[:, width:], TN)
            return dot(cu, z[:, :width], NN)

        total, held = None, front(0)
        for q in range(len(tiles)):
            now = held
            if q < len(tiles) - 1:
                held = front(q + 1)
            part = rear(q, *now)
            total = part if total is None else total + part
        PU[k] += total.reshape(4, 4, rows, width)

    halves = [(core, n) for core in range(2) for n in range(2)]

    def early(i, carry):
        @pl.when(i == 0)
        def _():
            arrive(second[0])

        @pl.when(i == 1)
        def _():
            item_f[0].wait_recv()
            work(0, [(1, 0, 0), (1, 1, 0)])
            arrive(second[1])
            item_m[1].wait_recv()
            item_f[1].start()

        @pl.when(i == 2)
        def _():
            item_f[1].wait_recv()

        work(lax.div(i + 1, 2), [(lax.div(i, 2), *ch) for ch in halves])
        return carry

    def late(k, carry):
        for n in (2, 3):
            @pl.when(k == n)
            def _():
                arrive(second[n])

        work(k, [(side, *ch) for side in range(2) for ch in halves])
        for n in (2, 3):
            @pl.when(k == n)
            def _():
                out1(n)
        return carry

    item_m[0].wait_recv()
    item_f[0].start()
    lax.fori_loop(0, 3, early, 0)
    out1(1)
    lax.fori_loop(2, 4, late, 0)
    sum1(1)
    sum_s0.start()
    work(0, [(1, 1, 1), (1, 0, 1)])
    sum_s1.start()
    out1(0)
    sum1(2)
    sum_s1.wait_recv()
    code(PV[2] + RI1[1], QI, FI)
    begin(sum_m[:4])
    sum2(1)
    sum1(3)
    sum2(2)
    sum_m[4].start()
    sum1(0)
    sum2(3)
    for cp in gathers:
        cp.wait_send()
    sum2(0)
    out = 1.0 / 256.0
    sum_s0.wait_recv()
    arrive(sum_m)
    for l in lanes:
        OI[:, l] = (PV[0, :, l] + RI1[0, :, l] + plain(R4, E4, l)) * out
    away = [
        pltpu.make_async_copy(OU, ou, local.at[0]),
        pltpu.make_async_copy(OI, oi, local.at[1]),
    ]
    away[1].start()
    arrive(back3)
    for l in lanes:
        v = S2[0, :, l]
        for n in range(3):
            v += plain(R3.at[n], E3.at[n], l)
        OU[:, l] = v * out
    away[0].start()
    for cp in made[len(gathers) :]:
        cp.wait_send()
    for cp in away:
        cp.wait()


def on_device(user_factors, item_factors, user_tangent, item_tangent, block_mask):
    rows, width = user_factors.shape
    items = item_factors.shape[0]
    f32, bf16 = jnp.float32, jnp.bfloat16
    scratch = [
        pltpu.VMEM((4, 4, 4, rows, 2 * width), bf16),
        pltpu.VMEM((4, items, 2 * width), bf16),
        pltpu.VMEM(block_mask.shape, jnp.int32),
        pltpu.VMEM((2, 4, 8, 128), f32),
        pltpu.VMEM((4, 2, 16, 8, 2 * items), f32),
        pltpu.VMEM((4, 4, 4, rows, width), f32),
        pltpu.VMEM((4, items, width), f32),
        pltpu.VMEM((4, 2, 3, 4, rows // 2, width), jnp.int16),
        pltpu.VMEM((4, 2, 3, 8, 128), f32),
        pltpu.VMEM((4, 2, 3, 4, rows // 2, width), jnp.int16),
        pltpu.VMEM((4, 2, 3, 8, 128), f32),
        pltpu.VMEM((4, 2, 4, rows // 2, width), f32),
        pltpu.VMEM((4, 2, 3, rows // 2, width), f32),
        pltpu.VMEM((4, rows, width), f32),
        pltpu.VMEM((3, rows, width), jnp.int16),
        pltpu.VMEM((3, 8, 128), f32),
        pltpu.VMEM((3, rows, width), jnp.int16),
        pltpu.VMEM((3, 8, 128), f32),
        pltpu.VMEM((2, items, width), f32),
        pltpu.VMEM((items, width), jnp.int16),
        pltpu.VMEM((8, 128), f32),
        pltpu.VMEM((items, width), jnp.int16),
        pltpu.VMEM((8, 128), f32),
        pltpu.VMEM((rows, width), f32),
        pltpu.VMEM((items, width), f32),
        pltpu.SemaphoreType.DMA((N_SEM,)),
        pltpu.SemaphoreType.DMA((N_SEM,)),
        pltpu.SemaphoreType.DMA((5,)),
    ]
    args = (user_factors, user_tangent, item_factors, item_tangent, block_mask)
    hbm = [pltpu.with_memory_space_constraint(a, pltpu.HBM) for a in args]
    return pl.pallas_call(
        kernel,
        out_shape=(
            jax.ShapeDtypeStruct((rows, width), f32),
            jax.ShapeDtypeStruct((items, width), f32),
        ),
        in_specs=[pl.BlockSpec(memory_space=pltpu.HBM)] * 5,
        out_specs=[pl.BlockSpec(memory_space=pl.ANY)] * 2,
        scratch_shapes=scratch,
        compiler_params=pltpu.CompilerParams(
            collective_id=0, has_side_effects=True, vmem_limit_bytes=40 << 20
        ),
    )(*hbm)


def solution(mesh):
    placed = (
        P(("au", "ia"), None),
        P(("ia", "au"), None),
        P(("au", "ia"), None),
        P(("ia", "au"), None),
        P("au", "ia"),
    )
    return jax.shard_map(
        on_device,
        mesh=mesh,
        in_specs=placed,
        out_specs=(P(("au", "ia"), None), P(("ia", "au"), None)),
        check_vma=False,
    )
```
